256 devices in a mesh: seq: 32 (over z, x), fsdp: 8 (over y, core).
Axes of the slice: x: 4, y: 4, z: 8, core: 2. Of those that a mesh axis runs over, the one named last changes fastest.
Arguments:
- tokens: bfloat16 [24576, 6144], P('seq'), may hold values from -30 to 30
- w_query: bfloat16 [6144, 32, 128], P('seq', 'fsdp'), may hold values from -0.078125 to 0.078125
- w_keyval: bfloat16 [6144, 32, 256], P('seq', 'fsdp'), may hold values from -40 to 40
- doc_lengths: int32 [8], replicated, may hold values from 1 to 12288, 24576 in all
- norm_gain: bfloat16 [4096], P('fsdp'), may hold values from 0.25 to 1.75
Outputs:
- attended: bfloat16 [24576, 4096], P('seq', 'fsdp')
The draws below stay inside these ranges and needn't reach their ends.
Inputs may be any that keep to these rules, and one draw needn't show every extreme that they name: `doc_lengths`: lengths are positive and sum to 24576; the longest document has exactly 12288 tokens.
All inputs are finite; a program needn't handle non-finite values.
Results may differ from the reference program's by a relative error of at most 0.0034.
Values may be sent and summed in bfloat16 or wider, within the bound.
A program may use at most 128 MiB of HBM per device.

```python
import math
import jax
import jax.numpy as jnp
import numpy as np
from jax import lax

D = 6144
H = 32
DH = 128
TOK_DEV = 768
NDOCS = 8
TOKENS = 24576
N_SEQ = 32


def draw_tokens(key, part):
    first, second = jax.random.split(key)
    scales = jnp.exp(jax.random.uniform(first, (TOKENS, 1), jnp.float32, math.log(0.5), math.log(5.0)))
    entries = jnp.clip(jax.random.normal(second, (TOKENS, D), jnp.float32), -6.0, 6.0)
    return (entries * scales).astype(jnp.bfloat16)


def draw_w_keyval(key, part):
    first, second = jax.random.split(key)
    ramp = 10.0 ** (jnp.arange(H, dtype=jnp.float32) / (H - 1))
    jitter = jnp.exp(jax.random.uniform(second, (H,), jnp.float32, math.log(0.7), math.log(1.4)))
    entries = jnp.clip(jax.random.normal(first, (D, H, 2 * DH), jnp.float32), -4.0, 4.0)
    column = jnp.concatenate([jnp.ones((H, DH), jnp.float32), (ramp * jitter)[:, None] * jnp.ones((1, DH), jnp.float32)], axis=1)
    return (entries * column[None] / math.sqrt(D)).astype(jnp.bfloat16)


def levels(stream_key, dims, cuts, low, top_value):
    loudness, own = 1.0, jax.random.fold_in(stream_key, 6)
    for axis_at, parts in cuts:
        heights = jnp.exp(jax.random.uniform(jax.random.fold_in(own, axis_at), (parts,), jnp.float32, low / len(cuts), top_value / len(cuts)))
        loudness = loudness * jnp.repeat(heights, dims[axis_at] // parts).reshape([-1 if axis == axis_at else 1 for axis in range(len(dims))])
    return loudness


def split_up(amount, total, bound, lean):
    weights = [(1 << 20) // math.isqrt(grade ** lean) + 1 for grade in range(2, amount + 1)]
    rest, given = total - bound - (amount - 1), [1] * (amount - 1)
    while rest > 0:
        free = [i for i in range(amount - 1) if given[i] < bound]
        whole, remaining = sum([weights[i] for i in free]), rest
        for i in free:
            addition = min(bound - given[i], max(1, remaining * weights[i] // whole), rest)
            given[i] = given[i] + addition
            rest = rest - addition
    return np.array([bound] + given)


def ragged(stream_key, count, total, reach, slope):
    if count == 2:
        one = jax.random.randint(stream_key, (), max(1, total - reach), min(reach, total - 1) + 1)
        return jnp.stack([one, total - one])
    lengths = jnp.asarray(split_up(count, total, reach, slope), jnp.int32)
    pairs = (count - 1) // 2
    source_of, taker = lengths[1:1 + 2 * pairs:2], lengths[2:2 + 2 * pairs:2]
    slack = jnp.minimum(source_of - 1, reach - taker)
    passed = jax.random.randint(jax.random.fold_in(stream_key, 1), (pairs,), 0, 1 << 20) % (slack + 1)
    lengths = lengths.at[1:1 + 2 * pairs:2].set(source_of - passed).at[2:2 + 2 * pairs:2].set(taker + passed)
    return lengths[jax.random.permutation(jax.random.fold_in(stream_key, 2), count)]


def bell_draw(key, extent, width, reach, pieces=(), kind=jnp.bfloat16):
    result = jax.random.normal(key, extent, jnp.float32) * width
    if len(pieces) > 0:
        result = levels(key, extent, pieces, -0.22, 0.18) * result
    return jnp.clip(result, min=-reach, max=reach).astype(kind)


def setup_inputs(seed: int = 0) -> dict:
    key_list = jax.random.split(jax.random.key(seed), 6)
    return {
        "tokens": draw_tokens(jax.random.fold_in(key_list[5], 71), 0),
        "w_query": bell_draw(key_list[1], (D, H, DH), D ** -0.5, 0.078125, ((0, 32), (1, 8))),
        "w_keyval": draw_w_keyval(jax.random.fold_in(key_list[5], 71), 0),
        "doc_lengths": ragged(key_list[3], NDOCS, TOKENS, TOKENS // 2, 2).astype(jnp.int32),
        "norm_gain": jnp.clip(1.0 + 0.15 * jax.random.normal(key_list[4], (H * DH,), jnp.float32), 0.25, 1.75).astype(jnp.bfloat16),
    }


def doc_index(positions, doc_ends):
    return lax.optimization_barrier(jnp.sum((positions[:, None] >= doc_ends[None, :]).astype(jnp.int32), axis=1)).astype(jnp.int32)

def reference(tokens, w_query, w_keyval, doc_lengths, norm_gain):
    high = lax.Precision.HIGHEST
    doc_ends = jnp.cumsum(doc_lengths).astype(jnp.int32)
    query_matrix = w_query.reshape(D, H * DH)
    keyval_matrix = w_keyval.reshape(D, H * 2 * DH)
    token_blocks = tokens.reshape(N_SEQ, TOK_DEV, D)
    offsets = jnp.arange(TOK_DEV, dtype=jnp.int32)
    ordered = offsets[:, None] >= offsets[None, :]

    def advance(carried_in, block_item):
        head_state, state_doc = carried_in
        token_block, block_index = block_item
        doc_ids = doc_index(block_index * TOK_DEV + offsets, doc_ends)
        queries = jax.nn.silu(jnp.dot(token_block, query_matrix, preferred_element_type=jnp.float32))
        queries = queries.astype(jnp.bfloat16).reshape(TOK_DEV, H, DH).astype(jnp.float32)
        keyval = jax.nn.silu(jnp.dot(token_block, keyval_matrix, preferred_element_type=jnp.float32))
        keyval = keyval.astype(jnp.bfloat16).reshape(TOK_DEV, H, 2 * DH).astype(jnp.float32)
        key_rows = keyval[:, :, :DH]
        values = keyval[:, :, DH:]
        same_doc = doc_ids[:, None] == doc_ids[None, :]
        causal = (ordered & same_doc).astype(jnp.float32)
        scores = jnp.einsum('thd,shd->hts', queries, key_rows, precision=high) * causal[None]
        weights = lax.optimization_barrier(scores.astype(jnp.bfloat16)).astype(jnp.float32)
        within = jnp.einsum('hts,she->the', weights, values, precision=high)
        state_rounded = lax.optimization_barrier(head_state.astype(jnp.bfloat16)).astype(jnp.float32)
        carried = jnp.einsum('thd,hde->the', queries, state_rounded, precision=high)
        carried = carried * (doc_ids == state_doc).astype(jnp.float32)[:, None, None]
        mixed = within + carried
        sum_squares = lax.optimization_barrier(jnp.sum(mixed * mixed, axis=(1, 2)))
        inverse_rms = lax.rsqrt(sum_squares / (H * DH) + 1e-06)
        output = (mixed.reshape(TOK_DEV, H * DH) * inverse_rms[:, None] * norm_gain.astype(jnp.float32)[None, :]).astype(jnp.bfloat16)
        tail_doc = doc_ids[TOK_DEV - 1]
        tail_mask = (doc_ids == tail_doc).astype(jnp.float32)
        tail_state = jnp.einsum('thd,the->hde', key_rows * tail_mask[:, None, None], values, precision=high)
        kept = (state_doc == tail_doc).astype(jnp.float32)
        return ((tail_state + kept * head_state, tail_doc), output)
    start = (jnp.zeros((H, DH, DH), jnp.float32), jnp.array(-1, dtype=jnp.int32))
    _, outputs = lax.scan(advance, start, (token_blocks, jnp.arange(N_SEQ, dtype=jnp.int32)))
    return outputs.reshape(TOKENS, H * DH)
```

```python
import functools

import jax
import jax.numpy as jnp
from jax import lax
from jax.experimental import pallas as pl
from jax.experimental.pallas import tpu as pltpu
from jax.sharding import Mesh, PartitionSpec as P

NZ, NX, NY, NC = 8, 4, 4, 2
UNITS = 6
ROWS = 192
PR = 80
QR = ROWS - PR
WID = 256
TOK = 768
DM = 6144
DH = 128
HEADS = 4
MESH = pl.DeviceIdType.MESH


def doc_ends(len_ref):
    ends, total = [], jnp.int32(0)
    for i in range(8):
        total = total + len_ref[i]
        ends.append(total)
    return ends


def start_of(position, ends):
    start = jnp.zeros_like(position)
    for end in ends:
        start = jnp.maximum(start, jnp.where(position >= end, end, 0))
    return start


def gather_kernel(
    len_ref, tok_hbm, w_hbm, qkv_ref, tails_ref,
    wbuf, tokv, acc, local_sem,
    px_s, px_r, qz_s, qz_r, pz_s, pz_r, qx_s, qx_r,
):
    mz, mx = lax.axis_index("z"), lax.axis_index("x")
    shard = mz * NX + mx
    ends = doc_ends(len_ref)

    own = pltpu.make_async_copy(w_hbm, wbuf.at[:, mz, mx], local_sem.at[0])
    own.start()
    tok_copy = pltpu.make_async_copy(tok_hbm, tokv, local_sem.at[1])
    tok_copy.start()

    def z_at(delta):
        return lax.rem(mz + delta + NZ, NZ)

    def x_at(delta):
        return lax.rem(mx + delta + NX, NX)

    barrier = pltpu.get_barrier_semaphore()
    for delta in (1, -1):
        pl.semaphore_signal(barrier, inc=1, device_id={"z": z_at(delta)}, device_id_type=MESH)
        pl.semaphore_signal(barrier, inc=1, device_id={"x": x_at(delta)}, device_id_type=MESH)
    pl.semaphore_wait(barrier, 4)
    own.wait()

    def copy(ref, send, recv, target):
        return pltpu.make_async_remote_copy(
            src_ref=ref, dst_ref=ref, send_sem=send, recv_sem=recv,
            device_id=target, device_id_type=MESH,
        )

    def px(u, d, s, lag):
        sign = 1 - 2 * d
        block = x_at(-sign * (s + lag))
        rows = (0, PR) if s == 0 else ((0, 48) if d == 0 else (48, 32))
        return copy(
            wbuf.at[u, mz, block, pl.ds(*rows), :], px_s.at[u, d, s], px_r.at[u, d, s],
            {"x": x_at(sign)},
        )

    def qz(u, d, s, lag):
        sign = 1 - 2 * d
        block = z_at(-sign * (s + lag))
        rows = (PR, QR) if s < 3 else ((PR, 48) if d == 0 else (PR + 48, QR - 48))
        return copy(
            wbuf.at[u, block, mx, pl.ds(*rows), :], qz_s.at[u, d, s], qz_r.at[u, d, s],
            {"z": z_at(sign)},
        )

    def pz(u, d, s, c, lag):
        sign = 1 - 2 * d
        block = z_at(-sign * (s + lag))
        return copy(
            wbuf.at[u, block, pl.ds(2 * c, 2), pl.ds(0, PR), :],
            pz_s.at[u, d, s, c], pz_r.at[u, d, s, c], {"z": z_at(sign)},
        )

    def qx(u, d, s, c, lag):
        sign = 1 - 2 * d
        block = x_at(-sign * (s + lag))
        return copy(
            wbuf.at[u, pl.ds(2 * c, 2), block, pl.ds(PR, QR), :],
            qx_s.at[u, d, s, c], qx_r.at[u, d, s, c], {"x": x_at(sign)},
        )

    qx_order = ((0, 1, 2, 3), (2, 3, 0, 1))

    def round_body(r, carry):
        n, p, c = r, r - 1, r - 2
        first, second, third = r < UNITS, (r >= 1) & (r <= UNITS), r >= 2

        def compute(step):
            lo = step * (DM // 4)
            part = jnp.dot(
                tokv[:, lo:lo + DM // 4],
                wbuf[c, 2 * step:2 * step + 2].reshape(DM // 4, WID),
                preferred_element_type=jnp.float32,
            )
            if step == 0:
                acc[...] = part
            else:
                acc[...] += part

        @pl.when(first)
        def _():
            for d in (0, 1):
                qz(n, d, 0, 0).start()
                px(n, d, 0, 0).start()

        @pl.when(second)
        def _():
            for d in (0, 1):
                px(p, d, 1, 1).wait_recv()
            for k in (0, 1):
                for d in (0, 1):
                    pz(p, d, 0, k, 0).start()
            for d in (0, 1):
                qz(p, d, 3, 1).wait_recv()
            for k in range(4):
                for d in (0, 1):
                    qx(p, d, 0, qx_order[d][k], 0).start()

        @pl.when(third)
        def _():
            pz(c, 0, 3, 0, 1).wait_recv()
            pz(c, 1, 3, 1, 1).wait_recv()
            for d in (0, 1):
                for k in (2, 3):
                    qx(c, d, 0, qx_order[d][k], 1).wait_recv()
                for k in (0, 1):
                    qx(c, d, 1, qx_order[d][k], 1).wait_recv()

        @pl.when(r == 2)
        def _():
            tok_copy.wait()

        @pl.when(third)
        def _():
            compute(0)

        for s in (1, 2, 3):
            @pl.when(first)
            def _():
                for d in (0, 1):
                    qz(n, d, s - 1, 1).wait_recv()
                    qz(n, d, s, 0).start()
                    if s == 1:
                        px(n, d, 0, 1).wait_recv()
                if s == 1:
                    for d in (0, 1):
                        px(n, d, 1, 0).start()

            @pl.when(second)
            def _():
                for k in (0, 1):
                    for d in (0, 1):
                        pz(p, d, s - 1, k, 1).wait_recv()
                        if s < 3 or k == d:
                            pz(p, d, s, k, 0).start()
                if s < 3:
                    for d in (0, 1):
                        qx(p, d, 0, qx_order[d][s - 1], 1).wait_recv()
                        qx(p, d, 1, qx_order[d][s - 1], 0).start()

            @pl.when(third)
            def _():
                compute(s)

        @pl.when(third)
        def _():
            total = acc[...]
            act = (total / (1.0 + jnp.exp(-total))).astype(jnp.bfloat16)
            qkv_ref[c] = act

            @pl.when(c < HEADS)
            def _():
                position = lax.broadcasted_iota(jnp.int32, (TOK, DH), 0) + shard * TOK
                last = start_of(shard * TOK + TOK - 1, ends)
                keys = act[:, :DH]
                kept = jnp.where(position >= last, keys, jnp.zeros_like(keys))
                tails_ref[c] = lax.dot_general(
                    kept, act[:, DH:], (((0,), (0,)), ((), ())),
                    preferred_element_type=jnp.float32,
                )

        return carry

    lax.fori_loop(0, UNITS + 2, round_body, 0)

    def drain(u, carry):
        for d in (0, 1):
            for s in (0, 1):
                px(u, d, s, 0).wait_send()
            for s in range(4):
                qz(u, d, s, 0).wait_send()
                for k in (0, 1):
                    if s < 3 or k == d:
                        pz(u, d, s, k, 0).wait_send()
            for k in range(4):
                qx(u, d, 0, qx_order[d][k], 0).wait_send()
                if k < 2:
                    qx(u, d, 1, qx_order[d][k], 0).wait_send()
        return carry

    lax.fori_loop(0, UNITS, drain, 0)


def attend_kernel(
    len_ref, qkv_ref, tails_ref, gain_ref, out_ref,
    t4, rt, inc_send, inc_recv, mixed, sums, inv_ref,
    ta_s, ta_r, rt_s, rt_r, ia_s, ia_r, sq_s, sq_r,
):
    mz, mx = lax.axis_index("z"), lax.axis_index("x")
    me = lax.axis_index("y") * NC + lax.axis_index("core")
    shard = mz * NX + mx
    ends = doc_ends(len_ref)

    def x_at(delta):
        return lax.rem(mx + delta + NX, NX)

    def z_at(delta):
        return lax.rem(mz + delta + NZ, NZ)

    def peer(delta):
        index = lax.rem(me + delta, NY * NC)
        return {"y": index // NC, "core": lax.rem(index, NC)}

    barrier = pltpu.get_barrier_semaphore()
    for k in range(1, NX):
        pl.semaphore_signal(barrier, inc=1, device_id={"x": x_at(k)}, device_id_type=MESH)
    for delta in (1, -1):
        pl.semaphore_signal(barrier, inc=1, device_id={"z": z_at(delta)}, device_id_type=MESH)
    for k in range(1, NY * NC):
        pl.semaphore_signal(barrier, inc=1, device_id=peer(k), device_id_type=MESH)
    pl.semaphore_wait(barrier, NX - 1 + 2 + NY * NC - 1)

    def copy(src, dst, send, recv, target):
        return pltpu.make_async_remote_copy(
            src_ref=src, dst_ref=dst, send_sem=send, recv_sem=recv,
            device_id=target, device_id_type=MESH,
        )

    def tail_to(k):
        return copy(tails_ref.at[x_at(k)], t4.at[mx], ta_s.at[k], ta_r.at[k], {"x": x_at(k)})

    def tail_from(k):
        return copy(tails_ref.at[mx], t4.at[x_at(-k)], ta_s.at[k], ta_r.at[k], {"x": x_at(k)})

    def relay(s):
        return copy(rt.at[s], rt.at[s + 1], rt_s.at[s], rt_r.at[s], {"z": z_at(1)})

    def inc_to(k):
        return copy(
            inc_send.at[x_at(k)], inc_recv.at[mx], ia_s.at[k], ia_r.at[k], {"x": x_at(k)}
        )

    def inc_from(k):
        return copy(
            inc_send.at[mx], inc_recv.at[x_at(-k)], ia_s.at[k], ia_r.at[k], {"x": x_at(k)}
        )

    def square_to(k):
        return copy(sums.at[0], sums.at[k], sq_s.at[k], sq_r.at[k], peer(k))

    for k in range(1, NX):
        tail_to(k).start()
    t4[mx] = tails_ref[mx]

    tile = 256
    base = shard * TOK

    def within(h):
        pos = h // 2
        off = (h % 2) * DH
        for i in range(TOK // tile):
            width = (i + 1) * tile
            q = qkv_ref[4 + pos, i * tile:(i + 1) * tile, off:off + DH]
            k = qkv_ref[h, 0:width, 0:DH]
            v = qkv_ref[h, 0:width, DH:2 * DH]
            scores = lax.dot_general(
                q, k, (((1,), (1,)), ((), ())), preferred_element_type=jnp.float32
            )
            t = lax.broadcasted_iota(jnp.int32, (tile, 1), 0) + (base + i * tile)
            begin = start_of(t, ends)
            s = lax.broadcasted_iota(jnp.int32, (1, width), 1) + base
            keep = (s <= t) & (s >= begin)
            weights = jnp.where(keep, scores, 0.0).astype(jnp.bfloat16)
            mixed[i * tile:(i + 1) * tile, h * DH:(h + 1) * DH] = jnp.dot(
                weights, v, preferred_element_type=jnp.float32
            )

    within(0)
    for k in range(1, NX):
        tail_from(k).wait_recv()
    row_last = start_of((mz + 1) * (NX * TOK) - 1, ends)
    total = jnp.zeros((DH, DH), jnp.float32)
    for j in range(NX):
        here = ((mz * NX + j + 1) * TOK - 1 >= row_last).astype(jnp.float32)
        total = total + here * t4[j]
    rt[0] = total
    within(1)
    relay(0).start()
    for s in (1, 2, 3):
        if s < 3:
            within(s + 1)
        relay(s - 1).wait_recv()
        relay(s).start()
    relay(3).wait_recv()

    row_first = start_of(mz * (NX * TOK), ends)
    before = jnp.zeros((DH, DH), jnp.float32)
    for d in range(1, 5):
        row = mz - d
        used = (row >= 0) & ((row + 1) * (NX * TOK) - 1 >= row_first)
        before = before + used.astype(jnp.float32) * rt[d]
    for j in range(NX):
        begin = start_of((mz * NX + j) * TOK, ends)
        state = (begin <= mz * (NX * TOK) - 1).astype(jnp.float32) * before
        for i in range(j):
            used = ((mz * NX + i + 1) * TOK - 1 >= begin).astype(jnp.float32)
            state = state + used * t4[i]
        inc_send[j] = state.astype(jnp.bfloat16)
    for k in range(1, NX):
        inc_to(k).start()
    inc_recv[mx] = inc_send[mx]
    for k in range(1, NX):
        inc_from(k).wait_recv()

    t = lax.broadcasted_iota(jnp.int32, (TOK, 1), 0) + base
    carried_on = (start_of(t, ends) <= base).astype(jnp.float32)
    squares = jnp.zeros((TOK, DH), jnp.float32)
    for h in range(HEADS):
        off = (h % 2) * DH
        q = qkv_ref[4 + h // 2, :, off:off + DH]
        carried = jnp.dot(q, inc_recv[h], preferred_element_type=jnp.float32)
        value = mixed[:, h * DH:(h + 1) * DH] + carried * carried_on
        mixed[:, h * DH:(h + 1) * DH] = value
        squares = squares + value * value
    for i in range(TOK // DH):
        flipped = squares[i * DH:(i + 1) * DH, :].T
        sums[0, i:i + 1, :] = jnp.sum(flipped, axis=0, keepdims=True)
    sums[0, 6:8, :] = jnp.zeros((2, DH), jnp.float32)
    for k in range(1, NY * NC):
        square_to(k).start()
    for k in range(1, NY * NC):
        square_to(k).wait_recv()
    total = sums[0]
    for k in range(1, NY * NC):
        total = total + sums[k]
    inv_ref[...] = lax.rsqrt(total / (HEADS * NY * NC * DH) + 1e-06)
    gain = gain_ref[...].astype(jnp.float32)
    for i in range(TOK // DH):
        scale = jnp.broadcast_to(inv_ref[i:i + 1, :], (DH, DH)).T
        for h in range(HEADS):
            value = mixed[i * DH:(i + 1) * DH, h * DH:(h + 1) * DH]
            out_ref[i * DH:(i + 1) * DH, h * DH:(h + 1) * DH] = (
                value * scale * gain[:, h * DH:(h + 1) * DH]
            ).astype(jnp.bfloat16)

    for k in range(1, NX):
        tail_to(k).wait_send()
        inc_to(k).wait_send()
    for s in range(4):
        relay(s).wait_send()
    for k in range(1, NY * NC):
        square_to(k).wait_send()


def shards(tokens, w_query, w_keyval, doc_lengths, norm_gain):
    units = [w_keyval[:, h, :] for h in range(HEADS)]
    units += [w_query[:, 2 * j:2 * j + 2, :].reshape(ROWS, WID) for j in range(2)]
    w_in = jnp.stack(units)
    dma = pltpu.SemaphoreType.DMA
    vmem = pl.BlockSpec(memory_space=pltpu.VMEM)
    smem = pl.BlockSpec(memory_space=pltpu.SMEM)
    anywhere = pl.BlockSpec(memory_space=pl.ANY)
    qkv, tails = pl.pallas_call(
        gather_kernel,
        out_shape=(
            jax.ShapeDtypeStruct((UNITS, TOK, WID), jnp.bfloat16),
            jax.ShapeDtypeStruct((HEADS, DH, DH), jnp.float32),
        ),
        in_specs=[smem, anywhere, anywhere],
        out_specs=(vmem, vmem),
        scratch_shapes=[
            pltpu.VMEM((UNITS, NZ, NX, ROWS, WID), jnp.bfloat16),
            pltpu.VMEM((TOK, DM), jnp.bfloat16),
            pltpu.VMEM((TOK, WID), jnp.float32),
            dma((2,)),
            dma((UNITS, 2, 2)), dma((UNITS, 2, 2)),
            dma((UNITS, 2, 4)), dma((UNITS, 2, 4)),
            dma((UNITS, 2, 4, 2)), dma((UNITS, 2, 4, 2)),
            dma((UNITS, 2, 2, 4)), dma((UNITS, 2, 2, 4)),
        ],
        compiler_params=pltpu.CompilerParams(
            collective_id=0, has_side_effects=True, vmem_limit_bytes=60 << 20
        ),
        name="gather",
    )(doc_lengths, tokens, w_in)
    peers = NY * NC
    return pl.pallas_call(
        attend_kernel,
        out_shape=jax.ShapeDtypeStruct((TOK, HEADS * DH), jnp.bfloat16),
        in_specs=[smem, vmem, vmem, vmem],
        out_specs=vmem,
        scratch_shapes=[
            pltpu.VMEM((NX, DH, DH), jnp.float32),
            pltpu.VMEM((5, DH, DH), jnp.float32),
            pltpu.VMEM((NX, DH, DH), jnp.bfloat16),
            pltpu.VMEM((NX, DH, DH), jnp.bfloat16),
            pltpu.VMEM((TOK, HEADS * DH), jnp.float32),
            pltpu.VMEM((peers, 8, DH), jnp.float32),
            pltpu.VMEM((8, DH), jnp.float32),
            dma((NX,)), dma((NX,)), dma((4,)), dma((4,)),
            dma((NX,)), dma((NX,)), dma((peers,)), dma((peers,)),
        ],
        compiler_params=pltpu.CompilerParams(
            collective_id=1, has_side_effects=True, vmem_limit_bytes=60 << 20
        ),
        name="attend",
    )(doc_lengths, qkv, tails, norm_gain.reshape(1, HEADS * DH))


def solution(mesh):
    grid = Mesh(mesh.devices.reshape(NZ, NX, NY, NC), ("z", "x", "y", "core"))
    seq, fsdp = ("z", "x"), ("y", "core")
    return jax.shard_map(
        shards,
        mesh=grid,
        in_specs=(P(seq, None), P(seq, fsdp, None), P(seq, fsdp, None), P(), P(fsdp)),
        out_specs=P(seq, fsdp),
        check_vma=False,
    )
```

```python
import jax
import jax.numpy as jnp
from jax import lax
from jax.experimental import pallas as pl
from jax.experimental.pallas import tpu as pltpu
from jax.sharding import Mesh, PartitionSpec as P

NZ, NX, NY, NC = 8, 4, 4, 2
PEERS = NY * NC
UNITS = 3
ROWS = 192
PR = 80
QR = ROWS - PR
WID = 256
TOK = 768
DM = 6144
DH = 128
PIECE = TOK // PEERS
SUB = PIECE // 3
TILE = 256
TILES = TOK // TILE
MESH = pl.DeviceIdType.MESH


def doc_ends(len_ref):
    ends, total = [], jnp.int32(0)
    for i in range(8):
        total = total + len_ref[i]
        ends.append(total)
    return ends


def start_of(position, ends):
    start = jnp.zeros_like(position)
    for end in ends:
        start = jnp.maximum(start, jnp.where(position >= end, end, 0))
    return start


def kernel(
    len_ref, tok_hbm, w_hbm, gain_ref, out_ref,
    wbuf, tbuf, tpb, tokv, acc, qkv, starts, tails, t4, rt, inc_send, inc,
    mixed, sums, osend, orecv, local_sem,
    pxm, pxp, pxf, qzm, qzt, pz, qxm, qxp, qxf, t1, t2, t3,
    ta, rl, ia, sq, oe,
):
    mz, mx = lax.axis_index("z"), lax.axis_index("x")
    my, mc = lax.axis_index("y"), lax.axis_index("core")
    me = my * NC + mc
    mate = mx + 1 - 2 * lax.rem(mx, 2)
    partner = NX - 1 - mx
    across = NX - 1 - mate
    group = mx // 2
    mine = lax.rem(mx, 2)
    ends = doc_ends(len_ref)
    blocks = (mz * NX + mx, mz * NX + partner)
    bases = (blocks[0] * TOK, blocks[1] * TOK)

    stage = (
        pltpu.make_async_copy(w_hbm.at[group], wbuf.at[:, mz, mx], local_sem.at[0]),
        pltpu.make_async_copy(
            w_hbm.at[1 - group, :, pl.ds(PR, QR), :], tbuf.at[:, mz], local_sem.at[1]
        ),
        pltpu.make_async_copy(w_hbm.at[1 - group, :, pl.ds(0, PR), :], tpb, local_sem.at[2]),
    )
    for item in stage:
        item.start()
    tok_copy = pltpu.make_async_copy(tok_hbm, tokv.at[0], local_sem.at[3])
    tok_copy.start()

    def z_at(delta):
        return lax.rem(mz + delta + NZ, NZ)

    def y_at(delta):
        return lax.rem(my + delta + NY, NY)

    def peer(side, k):
        index = lax.rem(me + k, PEERS)
        return {
            "x": mx if side == 0 else partner,
            "y": index // NC,
            "core": lax.rem(index, NC),
        }

    barrier = pltpu.get_barrier_semaphore()

    def greet(target):
        pl.semaphore_signal(barrier, inc=1, device_id=target, device_id_type=MESH)

    greet({"x": mate})
    greet({"z": z_at(1)})
    greet({"z": z_at(-1)})
    for k in range(PEERS):
        if k:
            greet(peer(0, k))
        greet(peer(1, k))
    pl.semaphore_wait(barrier, 3 + 2 * PEERS - 1)
    for item in stage:
        item.wait()

    def copy(src, dst, sems, index, target):
        return pltpu.make_async_remote_copy(
            src_ref=src, dst_ref=dst, send_sem=sems.at[(0, *index)],
            recv_sem=sems.at[(1, *index)], device_id=target, device_id_type=MESH,
        )

    def same(ref, sems, index, target):
        return copy(ref, ref, sems, index, target)

    to_mate, to_partner = {"x": mate}, {"x": partner}

    def upper(u, x):
        return wbuf.at[u, mz, x, pl.ds(0, PR), :]

    def px_mate(u, x):
        return same(upper(u, x), pxm, (u,), to_mate)

    def px_partner(u, x):
        return copy(tpb.at[u], upper(u, x), pxp, (u,), to_partner)

    def px_forward(u, x):
        return same(upper(u, x), pxf, (u,), to_mate)

    def qz(u, d, s, lag):
        sign = 1 - 2 * d
        block = z_at(-sign * (s + lag))
        lo, size = (0, QR) if s < 3 else ((0, 48) if d == 0 else (48, QR - 48))
        target = {"z": z_at(sign)}
        return (
            same(wbuf.at[u, block, mx, pl.ds(PR + lo, size), :], qzm, (u, d, s), target),
            same(tbuf.at[u, block, pl.ds(lo, size), :], qzt, (u, d, s), target),
        )

    def pzc(u, d, s, k, lag):
        sign = 1 - 2 * d
        block = z_at(-sign * (s + lag))
        return same(
            wbuf.at[u, block, pl.ds(2 * k, 2), pl.ds(0, PR), :],
            pz, (u, d, s, k), {"z": z_at(sign)},
        )

    def lower(u, k, x):
        return wbuf.at[u, pl.ds(2 * k, 2), x, pl.ds(PR, QR), :]

    def qx_mate(u, k, x):
        return same(lower(u, k, x), qxm, (u, k), to_mate)

    def qx_partner(u, k, x):
        return copy(tbuf.at[u, pl.ds(2 * k, 2)], lower(u, k, x), qxp, (u, k), to_partner)

    def qx_forward(u, k, x):
        return same(lower(u, k, x), qxf, (u, k), to_mate)

    def token_rows(y, core, j, half=None):
        start = (y * NC + core) * PIECE + j * SUB
        if half is None:
            return tokv.at[1, pl.ds(start, SUB), :]
        return tokv.at[1, pl.ds(start + half * (SUB // 2), SUB // 2), :]

    def tok_x(j):
        start = me * PIECE + j * SUB
        return copy(tok_hbm.at[pl.ds(start, SUB), :], token_rows(my, mc, j), t1, (j,), to_partner)

    def tok_y(j, d, s, lag):
        sign = 1 - 2 * d
        rows = token_rows(y_at(-sign * (s + lag)), mc, j, None if s == 0 else d)
        return same(rows, t2, (j, d, s), {"y": y_at(sign)})

    def tok_core(j, delta, receive):
        core = 1 - mc if receive else mc
        return same(token_rows(y_at(delta), core, j), t3, (j, delta % NY), {"core": 1 - mc})

    def tokens_in(j):
        tok_x(j).wait_recv()
        for d in (0, 1):
            tok_y(j, d, 0, 0).start()
        tok_core(j, 0, False).start()

    def tokens_hop(j):
        for d in (0, 1):
            tok_y(j, d, 0, 1).wait_recv()
            tok_y(j, d, 1, 0).start()
        for delta in (1, -1):
            tok_core(j, delta, False).start()

    def tokens_last(j):
        for d in (0, 1):
            tok_y(j, d, 1, 1).wait_recv()
        tok_core(j, 2, False).start()

    def tokens_end():
        for j in range(3):
            for delta in (0, 1, -1, 2):
                tok_core(j, delta, True).wait_recv()

    token_plan = {
        3: [(tokens_in, 0)], 5: [(tokens_in, 1)], 6: [(tokens_hop, 0)],
        7: [(tokens_hop, 1)], 8: [(tokens_in, 2), (tokens_last, 0)], 9: [(tokens_last, 1)],
        11: [(tokens_hop, 2)], 12: [(tokens_last, 2)],
    }

    def phase1_start(n):
        for d in (0, 1):
            for item in qz(n, d, 0, 0):
                item.start()
        px_partner(n, mx).start()
        px_mate(n, mx).start()

    def phase1_step(n, s):
        for d in (0, 1):
            for item in qz(n, d, s - 1, 1):
                item.wait_recv()
            for item in qz(n, d, s, 0):
                item.start()
        if s == 1:
            px_partner(n, partner).wait_recv()
            px_forward(n, partner).start()

    def phase2_start(p):
        px_mate(p, mate).wait_recv()
        px_forward(p, across).wait_recv()
        for k in (0, 1):
            for d in (0, 1):
                pzc(p, d, 0, k, 0).start()
        for d in (0, 1):
            for item in qz(p, d, 3, 1):
                item.wait_recv()
        for k in range(4):
            qx_partner(p, k, mx).start()
            qx_mate(p, k, mx).start()

    def phase2_step(p, s):
        for k in (0, 1):
            for d in (0, 1):
                pzc(p, d, s - 1, k, 1).wait_recv()
                if s < 3 or k == d:
                    pzc(p, d, s, k, 0).start()
        for k in ((0,), (1, 2), (3,))[s - 1]:
            qx_partner(p, k, partner).wait_recv()
            qx_forward(p, k, partner).start()

    def phase2_end(p):
        for d in (0, 1):
            pzc(p, d, 3, d, 1).wait_recv()
        for k in range(4):
            qx_mate(p, k, mate).wait_recv()
            qx_forward(p, k, across).wait_recv()

    def project(u, slot, lo, hi):
        if lo == 0:
            acc[...] = jnp.zeros_like(acc)

        def step(pair, carry):
            columns = pl.ds(pl.multiple_of(pair * (DM // 4), 128), DM // 4)
            acc[...] += jnp.dot(
                tokv[slot, :, columns],
                wbuf[u, pl.ds(2 * pair, 2)].reshape(DM // 4, WID),
                preferred_element_type=jnp.float32,
            )
            return carry

        lax.fori_loop(lo, hi, step, 0)

    def activate(u, slot):
        total = acc[...]
        act = (total / (1.0 + jnp.exp(-total))).astype(jnp.bfloat16)
        qkv[u, slot] = act
        if u < 2:
            position = lax.broadcasted_iota(jnp.int32, (TOK, DH), 0) + bases[slot]
            last = start_of(bases[slot] + TOK - 1, ends)
            keys = act[:, :DH]
            kept = jnp.where(position >= last, keys, jnp.zeros_like(keys))
            tails[u, slot] = lax.dot_general(
                kept, act[:, DH:], (((0,), (0,)), ((), ())),
                preferred_element_type=jnp.float32,
            )

    def tail_copy(slot, place):
        source = tails.at[1 - mine, slot]
        return copy(source, t4.at[place], ta, (slot,), to_mate)

    def relay(s):
        return copy(rt.at[s], rt.at[s + 1], rl, (s,), {"z": z_at(1)})

    def inc_copy(slot, receive):
        place = (mate, across)[slot]
        head = 1 - mine if receive else mine
        return copy(inc_send.at[place], inc.at[head, slot], ia, (slot,), to_mate)

    def square_copy(i, side, k):
        return copy(
            sums.at[i, 0], sums.at[i, side * PEERS + k], sq, (i, side, k), peer(side, k)
        )

    def out_copy(i):
        rows = pl.ds(i * TILE, TILE)
        return copy(osend.at[rows, :], orecv.at[rows, :], oe, (i,), to_partner)

    for step in range(16):
        r, s = step // 4, step % 4
        n, p, c = r, r - 1, r - 2
        if s == 0:
            if n < UNITS:
                phase1_start(n)
            if r == 0:
                tok_x(0).start()
                tok_x(1).start()
                for slot in (0, 1):
                    t = lax.broadcasted_iota(jnp.int32, (TOK, 1), 0) + bases[slot]
                    starts[slot] = start_of(t, ends)
            if p >= 0:
                phase2_start(p)
            if r == 1:
                tok_x(2).start()
            if c >= 0:
                phase2_end(c)
        else:
            if n < UNITS:
                phase1_step(n, s)
            if p >= 0:
                phase2_step(p, s)
        for action, j in token_plan.get(step, ()):
            action(j)
        if r == 2:
            if s == 0:
                tok_copy.wait()
            project(0, 0, s, s + 1)
            if s == 3:
                activate(0, 0)
        if step == 12:
            project(1, 0, 0, 4)
            activate(1, 0)
        if step == 13:
            tokens_end()
            project(0, 1, 0, 4)
            activate(0, 1)
        if step == 14:
            project(1, 1, 0, 4)
            activate(1, 1)
        if step == 15:
            tail_copy(0, mx).start()
            tail_copy(1, partner).start()
            for slot, place in ((0, mx), (1, partner)):
                t4[place] = tails[mine, slot]

    def within(j, slot):
        for i in range(TILES):
            rows, width = slice(i * TILE, (i + 1) * TILE), (i + 1) * TILE
            scores = lax.dot_general(
                qkv[2, slot, rows, j * DH:(j + 1) * DH], qkv[j, slot, 0:width, 0:DH],
                (((1,), (1,)), ((), ())), preferred_element_type=jnp.float32,
            )
            t = lax.broadcasted_iota(jnp.int32, (TILE, 1), 0) + (bases[slot] + i * TILE)
            s = lax.broadcasted_iota(jnp.int32, (1, width), 1) + bases[slot]
            keep = (s <= t) & (s >= starts[slot, rows])
            weights = jnp.where(keep, scores, 0.0).astype(jnp.bfloat16)
            mixed[slot, rows, j * DH:(j + 1) * DH] = jnp.dot(
                weights, qkv[j, slot, 0:width, DH:2 * DH], preferred_element_type=jnp.float32
            )

    phase2_end(2)
    tail_copy(0, mate).wait_recv()
    tail_copy(1, across).wait_recv()
    row_last = start_of((mz + 1) * (NX * TOK) - 1, ends)
    total = jnp.zeros((DH, DH), jnp.float32)
    for j in range(NX):
        here = ((mz * NX + j + 1) * TOK - 1 >= row_last).astype(jnp.float32)
        total = total + here * t4[j]
    rt[0] = total
    project(2, 0, 0, 4)
    activate(2, 0)
    relay(0).start()
    project(2, 1, 0, 4)
    activate(2, 1)
    relay(0).wait_recv()
    relay(1).start()
    within(0, 0)
    within(1, 0)
    relay(1).wait_recv()
    relay(2).start()
    within(0, 1)
    relay(2).wait_recv()
    relay(3).start()
    within(1, 1)
    relay(3).wait_recv()

    row_first = start_of(mz * (NX * TOK), ends)
    before = jnp.zeros((DH, DH), jnp.float32)
    for d in range(1, 5):
        row = mz - d
        used = (row >= 0) & ((row + 1) * (NX * TOK) - 1 >= row_first)
        before = before + used.astype(jnp.float32) * rt[d]
    for j in range(NX):
        begin = start_of((mz * NX + j) * TOK, ends)
        state = (begin <= mz * (NX * TOK) - 1).astype(jnp.float32) * before
        for i in range(j):
            used = ((mz * NX + i + 1) * TOK - 1 >= begin).astype(jnp.float32)
            state = state + used * t4[i]
        inc_send[j] = state.astype(jnp.bfloat16)
    for slot in (0, 1):
        inc_copy(slot, False).start()
    for slot, place in ((0, mx), (1, partner)):
        inc[mine, slot] = inc_send[place]
    for slot in (0, 1):
        inc_copy(slot, True).wait_recv()

    def finish_tile(i):
        rows = slice(i * TILE, (i + 1) * TILE)
        for slot in (0, 1):
            carried_on = (starts[slot, rows] <= bases[slot]).astype(jnp.float32)
            squares = jnp.zeros((TILE, DH), jnp.float32)
            for j in (0, 1):
                columns = slice(j * DH, (j + 1) * DH)
                carried = jnp.dot(
                    qkv[2, slot, rows, columns], inc[j, slot],
                    preferred_element_type=jnp.float32,
                )
                value = mixed[slot, rows, columns] + carried * carried_on
                mixed[slot, rows, columns] = value
                squares = squares + value * value
            for a in range(TILE // DH):
                flipped = squares[a * DH:(a + 1) * DH, :].T
                sums[i, 0, slot, a:a + 1, :] = jnp.sum(flipped, axis=0, keepdims=True)
        for side in (0, 1):
            for k in range(PEERS):
                if side or k:
                    square_copy(i, side, k).start()

    gain = gain_ref[:, pl.ds(pl.multiple_of(group * WID, WID), WID)].astype(jnp.float32)
    own_columns = pl.ds(pl.multiple_of(group * WID, WID), WID)
    other_columns = pl.ds(pl.multiple_of((1 - group) * WID, WID), WID)

    def norm_tile(i):
        for side in (0, 1):
            for k in range(PEERS):
                if side or k:
                    square_copy(i, side, k).wait_recv()
        for slot in (1, 0):
            for a in range(TILE // DH):
                total = jnp.zeros((1, DH), jnp.float32)
                for side in (0, 1):
                    for k in range(PEERS):
                        part = sums[i, side * PEERS + k, slot if side == 0 else 1 - slot]
                        total = total + part[a:a + 1, :]
                scale = lax.rsqrt(total / (PEERS * 4 * DH) + 1e-06)
                scale = jnp.broadcast_to(scale, (DH, DH)).T
                rows = slice(i * TILE + a * DH, i * TILE + (a + 1) * DH)
                value = mixed[slot, rows, :]
                value = jnp.concatenate(
                    [value[:, :DH] * scale, value[:, DH:] * scale], axis=1
                )
                value = (value * gain).astype(jnp.bfloat16)
                if slot == 1:
                    osend[rows, :] = value
                else:
                    out_ref[rows, own_columns] = value

    for i in range(TILES):
        finish_tile(i)
    for i in range(TILES):
        norm_tile(i)
        out_copy(i).start()
    for i in range(TILES):
        rows = slice(i * TILE, (i + 1) * TILE)
        out_copy(i).wait_recv()
        out_ref[rows, other_columns] = orecv[rows, :]

    for u in range(UNITS):
        px_mate(u, mx).wait_send()
        px_partner(u, mx).wait_send()
        px_forward(u, partner).wait_send()
        for d in (0, 1):
            for s in range(4):
                for item in qz(u, d, s, 0):
                    item.wait_send()
                for k in (0, 1):
                    if s < 3 or k == d:
                        pzc(u, d, s, k, 0).wait_send()
        for k in range(4):
            qx_mate(u, k, mx).wait_send()
            qx_partner(u, k, mx).wait_send()
            qx_forward(u, k, partner).wait_send()
    for j in range(3):
        tok_x(j).wait_send()
        for d in (0, 1):
            tok_y(j, d, 0, 0).wait_send()
            tok_y(j, d, 1, 0).wait_send()
        for delta in (0, 1, -1, 2):
            tok_core(j, delta, False).wait_send()
    for slot in (0, 1):
        tail_copy(slot, mx).wait_send()
        inc_copy(slot, False).wait_send()
    for s in range(4):
        relay(s).wait_send()
    for i in range(TILES):
        out_copy(i).wait_send()
        for side in (0, 1):
            for k in range(PEERS):
                if side or k:
                    square_copy(i, side, k).wait_send()


def shards(tokens, w_query, w_keyval, doc_lengths, norm_gain):
    halves = []
    for g in (0, 1):
        halves += [w_keyval[:, 2 * g + j, :] for j in (0, 1)]
        halves.append(w_query[:, 2 * g:2 * g + 2, :].reshape(ROWS, WID))
    w_in = jnp.stack(halves).reshape(2, UNITS, ROWS, WID)
    vmem = pl.BlockSpec(memory_space=pltpu.VMEM)
    smem = pl.BlockSpec(memory_space=pltpu.SMEM)
    anywhere = pl.BlockSpec(memory_space=pl.ANY)

    def dma(*shape):
        return pltpu.SemaphoreType.DMA((2, *shape))

    f32, bf16 = jnp.float32, jnp.bfloat16
    return pl.pallas_call(
        kernel,
        out_shape=jax.ShapeDtypeStruct((TOK, 2 * WID), bf16),
        in_specs=[smem, anywhere, anywhere, vmem],
        out_specs=vmem,
        scratch_shapes=[
            pltpu.VMEM((UNITS, NZ, NX, ROWS, WID), bf16),
            pltpu.VMEM((UNITS, NZ, QR, WID), bf16),
            pltpu.VMEM((UNITS, PR, WID), bf16),
            pltpu.VMEM((2, TOK, DM), bf16),
            pltpu.VMEM((TOK, WID), f32),
            pltpu.VMEM((UNITS, 2, TOK, WID), bf16),
            pltpu.VMEM((2, TOK, 1), jnp.int32),
            pltpu.VMEM((2, 2, DH, DH), f32),
            pltpu.VMEM((NX, DH, DH), f32),
            pltpu.VMEM((5, DH, DH), f32),
            pltpu.VMEM((NX, DH, DH), bf16),
            pltpu.VMEM((2, 2, DH, DH), bf16),
            pltpu.VMEM((2, TOK, WID), f32),
            pltpu.VMEM((TILES, 2 * PEERS, 2, 8, DH), f32),
            pltpu.VMEM((TOK, WID), bf16),
            pltpu.VMEM((TOK, WID), bf16),
            pltpu.SemaphoreType.DMA((4,)),
            dma(UNITS), dma(UNITS), dma(UNITS),
            dma(UNITS, 2, 4), dma(UNITS, 2, 4), dma(UNITS, 2, 4, 2),
            dma(UNITS, 4), dma(UNITS, 4), dma(UNITS, 4),
            dma(3), dma(3, 2, 2), dma(3, 4),
            dma(2), dma(4), dma(2), dma(TILES, 2, PEERS), dma(TILES),
        ],
        compiler_params=pltpu.CompilerParams(
            collective_id=0, has_side_effects=True, vmem_limit_bytes=62 << 20
        ),
        name="layer",
    )(doc_lengths, tokens, w_in, norm_gain.reshape(1, 2 * WID))


def solution(mesh):
    grid = Mesh(mesh.devices.reshape(NZ, NX, NY, NC), ("z", "x", "y", "core"))
    seq, fsdp = ("z", "x"), ("y", "core")
    return jax.shard_map(
        shards,
        mesh=grid,
        in_specs=(P(seq, None), P(seq, fsdp, None), P(seq, fsdp, None), P(), P(fsdp)),
        out_specs=P(seq, fsdp),
        check_vma=False,
    )
```

```python
import jax
import jax.numpy as jnp
from jax import lax
from jax.experimental import pallas as pl
from jax.experimental.pallas import tpu as pltpu
from jax.sharding import Mesh, PartitionSpec as P

NZ, NX, NY, NC = 8, 4, 4, 2
PEERS = NY * NC
UNITS = 3
ROWS = 192
PR = 80
QR = ROWS - PR
WID = 256
TOK = 768
DM = 6144
DH = 128
PIECE = TOK // PEERS
SUBS = 6
SUB = PIECE // SUBS
STEPS = 16
TILE = 256
TILES = TOK // TILE
MESH = pl.DeviceIdType.MESH


def doc_ends(len_ref):
    ends, total = [], jnp.int32(0)
    for i in range(8):
        total = total + len_ref[i]
        ends.append(total)
    return ends


def start_of(position, ends):
    start = jnp.zeros_like(position)
    for end in ends:
        start = jnp.maximum(start, jnp.where(position >= end, end, 0))
    return start


def kernel(
    len_ref, tok_hbm, w_hbm, gain_ref, out_ref,
    wbuf, tbuf, tpb, tokv, acc, qkv, starts, tails, t4, rt, inc_send, inc,
    mixed, sums, sends, osend, orecv, local_sem,
    pxm, pxp, pxf, qzm, qzt, pz, qxm, qxp, qxf, t1, t2, t3,
    ta, rl, ia, sq, oe,
):
    mz, mx = lax.axis_index("z"), lax.axis_index("x")
    my, mc = lax.axis_index("y"), lax.axis_index("core")
    me = my * NC + mc
    mate = mx + 1 - 2 * lax.rem(mx, 2)
    partner = NX - 1 - mx
    across = NX - 1 - mate
    group = mx // 2
    mine = lax.rem(mx, 2)
    ends = doc_ends(len_ref)
    blocks = (mz * NX + mx, mz * NX + partner)
    bases = (blocks[0] * TOK, blocks[1] * TOK)

    stage = (
        pltpu.make_async_copy(w_hbm.at[group], wbuf.at[:, mz, mx], local_sem.at[0]),
        pltpu.make_async_copy(
            w_hbm.at[1 - group, :, pl.ds(PR, QR), :], tbuf.at[:, mz], local_sem.at[1]
        ),
        pltpu.make_async_copy(w_hbm.at[1 - group, :, pl.ds(0, PR), :], tpb, local_sem.at[2]),
    )
    for item in stage:
        item.start()
    tok_copy = pltpu.make_async_copy(tok_hbm, tokv.at[0], local_sem.at[3])
    tok_copy.start()

    def z_at(delta):
        return lax.rem(mz + delta + NZ, NZ)

    def y_at(delta):
        return lax.rem(my + delta + NY, NY)

    def peer(side, k):
        index = lax.rem(me + k, PEERS)
        return {
            "x": mx if side == 0 else partner,
            "y": index // NC,
            "core": lax.rem(index, NC),
        }

    barrier = pltpu.get_barrier_semaphore()

    def greet(target):
        pl.semaphore_signal(barrier, inc=1, device_id=target, device_id_type=MESH)

    greet({"x": mate})
    for delta in (1, -1, 3, -3):
        greet({"z": z_at(delta)})
    for k in range(PEERS):
        if k:
            greet(peer(0, k))
        greet(peer(1, k))
    pl.semaphore_wait(barrier, 5 + 2 * PEERS - 1)
    for item in stage:
        item.wait()

    def copy(src, dst, sems, index, target):
        return pltpu.make_async_remote_copy(
            src_ref=src, dst_ref=dst, send_sem=sems.at[(0, *index)],
            recv_sem=sems.at[(1, *index)], device_id=target, device_id_type=MESH,
        )

    def same(ref, sems, index, target):
        return copy(ref, ref, sems, index, target)

    to_mate, to_partner = {"x": mate}, {"x": partner}

    def upper(u, x):
        return wbuf.at[u, mz, x, pl.ds(0, PR), :]

    def px_mate(u, x):
        return same(upper(u, x), pxm, (u,), to_mate)

    def px_partner(u, x):
        return copy(tpb.at[u], upper(u, x), pxp, (u,), to_partner)

    def px_forward(u, x):
        return same(upper(u, x), pxf, (u,), to_mate)

    def qz(u, d, s, lag):
        sign = 1 - 2 * d
        block = z_at(-sign * (s + lag))
        lo, size = (0, QR) if s < 3 else ((0, 48) if d == 0 else (48, QR - 48))
        target = {"z": z_at(sign)}
        return (
            same(wbuf.at[u, block, mx, pl.ds(PR + lo, size), :], qzm, (u, d, s), target),
            same(tbuf.at[u, block, pl.ds(lo, size), :], qzt, (u, d, s), target),
        )

    def pzc(u, d, s, k, lag):
        sign = 1 - 2 * d
        block = z_at(-sign * (s + lag))
        pair = group if k == 0 else 1 - group
        return same(
            wbuf.at[u, block, pl.ds(2 * pair, 2), pl.ds(0, PR), :],
            pz, (u, d, s, k), {"z": z_at(sign)},
        )

    def block_at(i):
        if i == 0:
            return mz
        distance = (i + 1) // 2
        return z_at(-distance if i % 2 else distance)

    def lower(u, i, x):
        return wbuf.at[u, block_at(i), x, pl.ds(PR, QR), :]

    def qx_mate(u, i, x):
        return same(lower(u, i, x), qxm, (u, i), to_mate)

    def qx_partner(u, i, x):
        return copy(tbuf.at[u, block_at(i)], lower(u, i, x), qxp, (u, i), to_partner)

    def qx_forward(u, i, x):
        return same(lower(u, i, x), qxf, (u, i), to_mate)

    def token_rows(y, core, j):
        return tokv.at[1, pl.ds((y * NC + core) * PIECE + j * SUB, SUB), :]

    def tok_x(j):
        start = me * PIECE + j * SUB
        return copy(tok_hbm.at[pl.ds(start, SUB), :], token_rows(my, mc, j), t1, (j,), to_partner)

    def tok_y(j, d, s, lag):
        sign = 1 - 2 * d
        return same(
            token_rows(y_at(-sign * (s + lag)), mc, j), t2, (j, d, s), {"y": y_at(sign)}
        )

    def tok_core(j, delta, receive):
        core = 1 - mc if receive else mc
        return same(token_rows(y_at(delta), core, j), t3, (j, delta % NY), {"core": 1 - mc})

    def tokens_in(j):
        tok_x(j).wait_recv()
        for d in (0, 1):
            tok_y(j, d, 0, 0).start()
        tok_core(j, 0, False).start()

    def tokens_hop(j):
        for d in (0, 1):
            tok_y(j, d, 0, 1).wait_recv()
        tok_y(j, j % 2, 1, 0).start()
        for delta in (1, -1):
            tok_core(j, delta, False).start()

    def tokens_last(j):
        tok_y(j, j % 2, 1, 1).wait_recv()
        tok_core(j, 2, False).start()

    def tokens_end():
        for j in range(SUBS):
            for delta in (0, 1, -1, 2):
                tok_core(j, delta, True).wait_recv()

    token_plan = {
        2: [(tokens_in, 0)], 3: [(tokens_in, 1), (tokens_in, 2)],
        4: [(tokens_in, 3), (tokens_hop, 0)], 5: [(tokens_in, 4), (tokens_hop, 1)],
        6: [(tokens_in, 5), (tokens_last, 0), (tokens_hop, 2)],
        7: [(tokens_last, 1), (tokens_hop, 3)], 8: [(tokens_last, 2), (tokens_hop, 4)],
        9: [(tokens_last, 3), (tokens_hop, 5)], 10: [(tokens_last, 4), (tokens_last, 5)],
    }
    token_sends = {0: (0, 1), 1: (2,), 2: (3,), 3: (4,), 4: (5,)}

    def arrivals(step):
        return {0: (0,), 1: (1, 2), 2: (3, 4), 3: (5, 6), 4: (7,)}.get(step, ())

    def events(u, s):
        lag = 1 if u < 2 else 0
        if s == 0:
            px_partner(u, mx).start()
            px_mate(u, mx).start()
        if 1 <= s <= 4:
            for d in (0, 1):
                for item in qz(u, d, s - 1, 1):
                    item.wait_recv()
        if s <= 3:
            for d in (0, 1):
                for item in qz(u, d, s, 0):
                    item.start()
        for i in arrivals(s):
            qx_partner(u, i, mx).start()
            qx_mate(u, i, mx).start()
        if s == 1:
            px_partner(u, partner).wait_recv()
            px_forward(u, partner).start()
        for k in (0, 1):
            hop = s - 1 - k
            if hop == 0:
                if k == 0:
                    px_mate(u, mate).wait_recv()
                else:
                    px_forward(u, across).wait_recv()
            for d in (0, 1):
                if 1 <= hop <= 3 or (hop == 4 and k == d):
                    pzc(u, d, hop - 1, k, 1).wait_recv()
                if 0 <= hop <= 2 or (hop == 3 and k == d):
                    pzc(u, d, hop, k, 0).start()
        for i in arrivals(s - 2 - lag):
            qx_partner(u, i, partner).wait_recv()
            qx_forward(u, i, partner).start()

    def arrived(u, group_at):
        for i in arrivals(group_at):
            qx_mate(u, i, mate).wait_recv()
            qx_forward(u, i, across).wait_recv()

    def product(u, slot, block):
        columns = pl.ds(pl.multiple_of(block * (DM // NZ), DH), DM // NZ)
        return jnp.dot(
            tokv[slot, :, columns], wbuf[u, block].reshape(DM // NZ, WID),
            preferred_element_type=jnp.float32,
        )

    def project(u, slots, group_at):
        if group_at == 0:
            for slot in slots:
                acc[slot] = product(u, slot, mz)
            return
        sides = len(arrivals(group_at))

        def step(index, carry):
            slot = index // sides if len(slots) == 2 else slots[0]
            sign = 1 - 2 * lax.rem(index, sides)
            acc[slot] += product(u, slot, lax.rem(mz + sign * group_at + NZ, NZ))
            return carry

        lax.fori_loop(0, sides * len(slots), step, 0)

    def project_all(u, slot):
        acc[slot] = product(u, slot, 0)

        def step(block, carry):
            acc[slot] += product(u, slot, block)
            return carry

        lax.fori_loop(1, NZ, step, 0)

    def activate(u, slot):
        total = acc[slot]
        act = (total / (1.0 + jnp.exp(-total))).astype(jnp.bfloat16)
        qkv[u, slot] = act
        if u < 2:
            position = lax.broadcasted_iota(jnp.int32, (TOK, DH), 0) + bases[slot]
            last = start_of(bases[slot] + TOK - 1, ends)
            keys = act[:, :DH]
            kept = jnp.where(position >= last, keys, jnp.zeros_like(keys))
            tails[u, slot] = lax.dot_general(
                kept, act[:, DH:], (((0,), (0,)), ((), ())),
                preferred_element_type=jnp.float32,
            )

    def tail_copy(slot, place):
        source = tails.at[1 - mine, slot]
        return copy(source, t4.at[place], ta, (slot,), to_mate)

    def relay(s):
        if s == 0:
            return copy(rt.at[0], rt.at[1], rl, (0,), {"z": z_at(1)})
        return copy(rt.at[2], rt.at[2 + s], rl, (s,), {"z": z_at(1 if s == 1 else 3)})

    def inc_copy(slot, receive):
        place = (mate, across)[slot]
        head = 1 - mine if receive else mine
        return copy(inc_send.at[place], inc.at[head, slot], ia, (slot,), to_mate)

    def square_copy(side, k):
        return copy(
            sends.at[side], sums.at[side * PEERS + k], sq, (side, k), peer(side, k)
        )

    def out_copy(i):
        rows = pl.ds(i * TILE, TILE)
        return copy(osend.at[rows, :], orecv.at[rows, :], oe, (i,), to_partner)

    def row_tail():
        tail_copy(0, mate).wait_recv()
        tail_copy(1, across).wait_recv()
        row_last = start_of((mz + 1) * (NX * TOK) - 1, ends)
        total = jnp.zeros((DH, DH), jnp.float32)
        for j in range(NX):
            here = ((mz * NX + j + 1) * TOK - 1 >= row_last).astype(jnp.float32)
            total = total + here * t4[j]
        rt[0] = total

    def row_pair():
        relay(0).wait_recv()
        row_last = start_of((mz + 1) * (NX * TOK) - 1, ends)
        kept = (mz >= 1) & (mz * (NX * TOK) - 1 >= row_last)
        rt[2] = rt[0] + kept.astype(jnp.float32) * rt[1]

    for step in range(STEPS):
        for u in reversed(range(UNITS)):
            if 0 <= step - 4 * u <= 7:
                events(u, step - 4 * u)
        for j in token_sends.get(step, ()):
            tok_x(j).start()
        for action, j in token_plan.get(step, ()):
            action(j)
        if step == 13:
            tail_copy(0, mx).start()
            tail_copy(1, partner).start()
        if step == 14:
            relay(0).start()
        if step == 15:
            relay(1).start()
            relay(2).start()
        if step == 0:
            for slot in (0, 1):
                t = lax.broadcasted_iota(jnp.int32, (TOK, 1), 0) + bases[slot]
                starts[slot] = start_of(t, ends)
        if step == 4:
            tok_copy.wait()
        for u in (0, 1):
            part = step - 4 * u - 4
            if 0 <= part <= 4:
                arrived(u, part)
                project(u, (0,), part)
                if part == 4:
                    activate(u, 0)
        if step == 11:
            tokens_end()
            project_all(0, 1)
            activate(0, 1)
        if step == 12:
            project_all(1, 1)
            activate(1, 1)
            parts = (0, 1)
        else:
            parts = (step - 11,) if step > 12 else ()
        for part in parts:
            arrived(2, part)
            project(2, (1, 0), part)
        if step == 13:
            for slot, place in ((0, mx), (1, partner)):
                t4[place] = tails[mine, slot]
            row_tail()
        if step == 14:
            row_pair()
    activate(2, 1)
    activate(2, 0)

    def within(j, slot):
        for i in range(TILES):
            rows, width = slice(i * TILE, (i + 1) * TILE), (i + 1) * TILE
            scores = lax.dot_general(
                qkv[2, slot, rows, j * DH:(j + 1) * DH], qkv[j, slot, 0:width, 0:DH],
                (((1,), (1,)), ((), ())), preferred_element_type=jnp.float32,
            )
            t = lax.broadcasted_iota(jnp.int32, (TILE, 1), 0) + (bases[slot] + i * TILE)
            s = lax.broadcasted_iota(jnp.int32, (1, width), 1) + bases[slot]
            keep = (s <= t) & (s >= starts[slot, rows])
            weights = jnp.where(keep, scores, 0.0).astype(jnp.bfloat16)
            mixed[slot, rows, j * DH:(j + 1) * DH] = jnp.dot(
                weights, qkv[j, slot, 0:width, DH:2 * DH], preferred_element_type=jnp.float32
            )

    for slot in (1, 0):
        within(0, slot)
        within(1, slot)
    relay(1).wait_recv()
    relay(2).wait_recv()
    row_first = start_of(mz * (NX * TOK), ends)
    before = jnp.zeros((DH, DH), jnp.float32)
    for d, at in ((1, 3), (3, 4)):
        row = mz - d
        used = (row >= 0) & ((row + 1) * (NX * TOK) - 1 >= row_first)
        before = before + used.astype(jnp.float32) * rt[at]
    for j in range(NX):
        begin = start_of((mz * NX + j) * TOK, ends)
        state = (begin <= mz * (NX * TOK) - 1).astype(jnp.float32) * before
        for i in range(j):
            used = ((mz * NX + i + 1) * TOK - 1 >= begin).astype(jnp.float32)
            state = state + used * t4[i]
        inc_send[j] = state.astype(jnp.bfloat16)
    for slot in (0, 1):
        inc_copy(slot, False).start()
    for slot, place in ((0, mx), (1, partner)):
        inc[mine, slot] = inc_send[place]
    for slot in (0, 1):
        inc_copy(slot, True).wait_recv()

    def finish_tile(slot, i):
        rows = slice(i * TILE, (i + 1) * TILE)
        carried_on = (starts[slot, rows] <= bases[slot]).astype(jnp.float32)
        squares = jnp.zeros((TILE, DH), jnp.float32)
        for j in (0, 1):
            columns = slice(j * DH, (j + 1) * DH)
            carried = jnp.dot(
                qkv[2, slot, rows, columns], inc[j, slot], preferred_element_type=jnp.float32
            )
            value = mixed[slot, rows, columns] + carried * carried_on
            if slot == 0:
                mixed[slot, rows, columns] = value
            else:
                osend[rows, columns] = value.astype(jnp.bfloat16)
            squares = squares + value * value
        for a in range(TILE // DH):
            flipped = squares[a * DH:(a + 1) * DH, :].T
            row = i * (TILE // DH) + a
            sends[slot, row:row + 1, :] = jnp.sum(flipped, axis=0, keepdims=True)

    for slot in (0, 1):
        sends[slot, TOK // DH:8, :] = jnp.zeros((8 - TOK // DH, DH), jnp.float32)
    for i in range(TILES):
        finish_tile(1, i)
        if i:
            out_copy(i - 1).start()
    for k in range(PEERS):
        square_copy(1, k).start()
    out_copy(TILES - 1).start()
    for i in range(TILES):
        finish_tile(0, i)
    for k in range(1, PEERS):
        square_copy(0, k).start()
    gain = gain_ref[...].astype(jnp.float32)
    own_columns = pl.ds(pl.multiple_of(group * WID, WID), WID)
    other_columns = pl.ds(pl.multiple_of((1 - group) * WID, WID), WID)
    is_first = (group == 0).astype(jnp.float32)
    own_gain = gain[:, :WID] * is_first + gain[:, WID:] * (1.0 - is_first)
    other_gain = gain[:, WID:] * is_first + gain[:, :WID] * (1.0 - is_first)
    for side in (0, 1):
        for k in range(PEERS):
            if side or k:
                square_copy(side, k).wait_recv()
    total = sends[0]
    for index in range(1, 2 * PEERS):
        total = total + sums[index]
    inverse = lax.rsqrt(total / (PEERS * 4 * DH) + 1e-06)
    scales = [
        jnp.broadcast_to(inverse[a:a + 1, :], (DH, DH)).T for a in range(TOK // DH)
    ]

    def write(columns, source, factor, a):
        rows = slice(a * DH, (a + 1) * DH)
        value = source[rows, :].astype(jnp.float32)
        value = jnp.concatenate(
            [value[:, :DH] * scales[a], value[:, DH:] * scales[a]], axis=1
        )
        out_ref[rows, columns] = (value * factor).astype(jnp.bfloat16)

    for a in range(TOK // DH):
        write(own_columns, mixed.at[0], own_gain, a)
    for i in range(TILES):
        out_copy(i).wait_recv()
        for a in (2 * i, 2 * i + 1):
            write(other_columns, orecv, other_gain, a)

    for u in range(UNITS):
        px_mate(u, mx).wait_send()
        px_partner(u, mx).wait_send()
        px_forward(u, partner).wait_send()
        for d in (0, 1):
            for s in range(4):
                for item in qz(u, d, s, 0):
                    item.wait_send()
                for k in (0, 1):
                    if s < 3 or k == d:
                        pzc(u, d, s, k, 0).wait_send()
        for i in range(NZ):
            qx_mate(u, i, mx).wait_send()
            qx_partner(u, i, mx).wait_send()
            qx_forward(u, i, partner).wait_send()
    for j in range(SUBS):
        tok_x(j).wait_send()
        for d in (0, 1):
            tok_y(j, d, 0, 0).wait_send()
        tok_y(j, j % 2, 1, 0).wait_send()
        for delta in (0, 1, -1, 2):
            tok_core(j, delta, False).wait_send()
    for slot in (0, 1):
        tail_copy(slot, mx).wait_send()
        inc_copy(slot, False).wait_send()
    for s in range(3):
        relay(s).wait_send()
    for i in range(TILES):
        out_copy(i).wait_send()
    for side in (0, 1):
        for k in range(PEERS):
            if side or k:
                square_copy(side, k).wait_send()


def shards(tokens, w_query, w_keyval, doc_lengths, norm_gain):
    halves = []
    for g in (0, 1):
        halves += [w_keyval[:, 2 * g + j, :] for j in (0, 1)]
        halves.append(w_query[:, 2 * g:2 * g + 2, :].reshape(ROWS, WID))
    w_in = jnp.stack(halves).reshape(2, UNITS, ROWS, WID)
    vmem = pl.BlockSpec(memory_space=pltpu.VMEM)
    smem = pl.BlockSpec(memory_space=pltpu.SMEM)
    anywhere = pl.BlockSpec(memory_space=pl.ANY)

    def dma(*shape):
        return pltpu.SemaphoreType.DMA((2, *shape))

    f32, bf16 = jnp.float32, jnp.bfloat16
    return pl.pallas_call(
        kernel,
        out_shape=jax.ShapeDtypeStruct((TOK, 2 * WID), bf16),
        in_specs=[smem, anywhere, anywhere, vmem],
        out_specs=vmem,
        scratch_shapes=[
            pltpu.VMEM((UNITS, NZ, NX, ROWS, WID), bf16),
            pltpu.VMEM((UNITS, NZ, QR, WID), bf16),
            pltpu.VMEM((UNITS, PR, WID), bf16),
            pltpu.VMEM((2, TOK, DM), bf16),
            pltpu.VMEM((2, TOK, WID), f32),
            pltpu.VMEM((UNITS, 2, TOK, WID), bf16),
            pltpu.VMEM((2, TOK, 1), jnp.int32),
            pltpu.VMEM((2, 2, DH, DH), f32),
            pltpu.VMEM((NX, DH, DH), f32),
            pltpu.VMEM((5, DH, DH), f32),
            pltpu.VMEM((NX, DH, DH), bf16),
            pltpu.VMEM((2, 2, DH, DH), bf16),
            pltpu.VMEM((2, TOK, WID), f32),
            pltpu.VMEM((2 * PEERS, 8, DH), f32),
            pltpu.VMEM((2, 8, DH), f32),
            pltpu.VMEM((TOK, WID), bf16),
            pltpu.VMEM((TOK, WID), bf16),
            pltpu.SemaphoreType.DMA((4,)),
            dma(UNITS), dma(UNITS), dma(UNITS),
            dma(UNITS, 2, 4), dma(UNITS, 2, 4), dma(UNITS, 2, 4, 2),
            dma(UNITS, NZ), dma(UNITS, NZ), dma(UNITS, NZ),
            dma(SUBS), dma(SUBS, 2, 2), dma(SUBS, NY),
            dma(2), dma(3), dma(2), dma(2, PEERS), dma(TILES),
        ],
        compiler_params=pltpu.CompilerParams(
            collective_id=0, has_side_effects=True, vmem_limit_bytes=62 << 20
        ),
        name="layer",
    )(doc_lengths, tokens, w_in, norm_gain.reshape(1, 2 * WID))


def solution(mesh):
    grid = Mesh(mesh.devices.reshape(NZ, NX, NY, NC), ("z", "x", "y", "core"))
    seq, fsdp = ("z", "x"), ("y", "core")
    return jax.shard_map(
        shards,
        mesh=grid,
        in_specs=(P(seq, None), P(seq, fsdp, None), P(seq, fsdp, None), P(), P(fsdp)),
        out_specs=P(seq, fsdp),
        check_vma=False,
    )
```

```python
import jax
import jax.numpy as jnp
from jax import lax
from jax.experimental import pallas as pl
from jax.experimental.pallas import tpu as pltpu
from jax.sharding import Mesh, PartitionSpec as P

NZ, NX, NY, NC = 8, 4, 4, 2
PEERS = NY * NC
UNITS = 3
ROWS = 192
PR = 80
QR = ROWS - PR
WID = 256
TOK = 768
DM = 6144
DH = 128
PIECE = TOK // PEERS
SUBS = 6
SUB = PIECE // SUBS
STEPS = 16
TILE = 256
TILES = TOK // TILE
MESH = pl.DeviceIdType.MESH


def doc_ends(len_ref):
    ends, total = [], jnp.int32(0)
    for i in range(8):
        total = total + len_ref[i]
        ends.append(total)
    return ends


def start_of(position, ends):
    start = jnp.zeros_like(position)
    for end in ends:
        start = jnp.maximum(start, jnp.where(position >= end, end, 0))
    return start


def kernel(
    len_ref, tok_hbm, wkv_hbm, wq_hbm, gain_ref, out_ref,
    wbuf, tbuf, tpb, tokv, acc, qkv, starts, tails, t4, rt, inc_send, inc,
    mixed, sums, sends, osend, orecv, local_sem,
    pxm, pxp, pxf, qzm, qzt, pz, qxm, qxp, qxf, t1, t2, t3,
    ta, rl, ia, sq, oe,
):
    mz, mx = lax.axis_index("z"), lax.axis_index("x")
    my, mc = lax.axis_index("y"), lax.axis_index("core")
    me = my * NC + mc
    mate = mx + 1 - 2 * lax.rem(mx, 2)
    partner = NX - 1 - mx
    across = NX - 1 - mate
    group = mx // 2
    mine = lax.rem(mx, 2)
    ends = doc_ends(len_ref)
    blocks = (mz * NX + mx, mz * NX + partner)
    bases = (blocks[0] * TOK, blocks[1] * TOK)

    def staged(index, source, target):
        return pltpu.make_async_copy(source, target, local_sem.at[index])

    kv_mine = wkv_hbm.at[pl.ds(2 * group, 2)]
    kv_other = wkv_hbm.at[pl.ds(2 * (1 - group), 2)]
    stage = [
        staged(0, kv_mine, wbuf.at[pl.ds(0, 2), mz, mx]),
        staged(1, kv_other.at[:, pl.ds(PR, QR), :], tbuf.at[pl.ds(0, 2), mz]),
        staged(2, kv_other.at[:, pl.ds(0, PR), :], tpb.at[pl.ds(0, 2)]),
    ]
    for j in (0, 1):
        columns = pl.ds(j * DH, DH)
        q_mine, q_other = wq_hbm.at[2 * group + j], wq_hbm.at[2 * (1 - group) + j]
        stage += [
            staged(4 + 3 * j, q_mine, wbuf.at[2, mz, mx, :, columns]),
            staged(5 + 3 * j, q_other.at[pl.ds(PR, QR), :], tbuf.at[2, mz, :, columns]),
            staged(6 + 3 * j, q_other.at[pl.ds(0, PR), :], tpb.at[2, :, columns]),
        ]
    for item in stage:
        item.start()
    tok_copy = pltpu.make_async_copy(tok_hbm, tokv.at[0], local_sem.at[3])
    tok_copy.start()

    def z_at(delta):
        return lax.rem(mz + delta + NZ, NZ)

    def y_at(delta):
        return lax.rem(my + delta + NY, NY)

    def peer(side, k):
        index = lax.rem(me + k, PEERS)
        return {
            "x": mx if side == 0 else partner,
            "y": index // NC,
            "core": lax.rem(index, NC),
        }

    barrier = pltpu.get_barrier_semaphore()

    def greet(target):
        pl.semaphore_signal(barrier, inc=1, device_id=target, device_id_type=MESH)

    greet({"x": mate})
    for delta in (1, -1, 3, -3):
        greet({"z": z_at(delta)})
    for k in range(PEERS):
        if k:
            greet(peer(0, k))
        greet(peer(1, k))
    pl.semaphore_wait(barrier, 5 + 2 * PEERS - 1)
    for item in stage:
        item.wait()

    def copy(src, dst, sems, index, target):
        return pltpu.make_async_remote_copy(
            src_ref=src, dst_ref=dst, send_sem=sems.at[(0, *index)],
            recv_sem=sems.at[(1, *index)], device_id=target, device_id_type=MESH,
        )

    def same(ref, sems, index, target):
        return copy(ref, ref, sems, index, target)

    def unit_copy(src, dst, sems, u, rest, target):
        return pltpu.make_async_remote_copy(
            src_ref=src, dst_ref=dst, send_sem=sems.at[(0, *rest)],
            recv_sem=sems.at[(1 + u, *rest)], device_id=target, device_id_type=MESH,
        )

    def unit_same(ref, sems, u, rest, target):
        return unit_copy(ref, ref, sems, u, rest, target)

    def send(make, u, *args):
        if u:
            make(u - 1, *args).wait_send()
        make(u, *args).start()

    to_mate, to_partner = {"x": mate}, {"x": partner}

    def upper(u, x):
        return wbuf.at[u, mz, x, pl.ds(0, PR), :]

    def px_mate(u, x):
        return unit_same(upper(u, x), pxm, u, (), to_mate)

    def px_partner(u, x):
        return unit_copy(tpb.at[u], upper(u, x), pxp, u, (), to_partner)

    def px_forward(u, x):
        return unit_same(upper(u, x), pxf, u, (), to_mate)

    def qz_part(d, s, lag):
        sign = 1 - 2 * d
        lo, size = (0, QR) if s < 3 else ((0, 48) if d == 0 else (48, QR - 48))
        return z_at(-sign * (s + lag)), lo, size, {"z": z_at(sign)}

    def qz_mine(u, d, s, lag):
        block, lo, size, target = qz_part(d, s, lag)
        return unit_same(wbuf.at[u, block, mx, pl.ds(PR + lo, size), :], qzm, u, (d, s), target)

    def qz_other(u, d, s, lag):
        block, lo, size, target = qz_part(d, s, lag)
        return unit_same(tbuf.at[u, block, pl.ds(lo, size), :], qzt, u, (d, s), target)

    def pzc(u, d, s, k, lag):
        sign = 1 - 2 * d
        block = z_at(-sign * (s + lag))
        pair = group if k == 0 else 1 - group
        return unit_same(
            wbuf.at[u, block, pl.ds(2 * pair, 2), pl.ds(0, PR), :],
            pz, u, (d, s, k), {"z": z_at(sign)},
        )

    def block_at(i):
        if i == 0:
            return mz
        distance = (i + 1) // 2
        return z_at(-distance if i % 2 else distance)

    def lower(u, i, x):
        return wbuf.at[u, block_at(i), x, pl.ds(PR, QR), :]

    def qx_mate(u, i, x):
        return unit_same(lower(u, i, x), qxm, u, (i,), to_mate)

    def qx_partner(u, i, x):
        return unit_copy(
            tbuf.at[u, block_at(i)], lower(u, i, x), qxp, u, (i,), to_partner
        )

    def qx_forward(u, i, x):
        return unit_same(lower(u, i, x), qxf, u, (i,), to_mate)

    def token_rows(y, core, j):
        return tokv.at[1, pl.ds((y * NC + core) * PIECE + j * SUB, SUB), :]

    def tok_x(j):
        start = me * PIECE + j * SUB
        return copy(tok_hbm.at[pl.ds(start, SUB), :], token_rows(my, mc, j), t1, (j,), to_partner)

    def tok_y(j, d, s, lag):
        sign = 1 - 2 * d
        return same(
            token_rows(y_at(-sign * (s + lag)), mc, j), t2, (j, 2 * s if s else d),
            {"y": y_at(sign)},
        )

    def tok_core(j, delta, receive):
        core = 1 - mc if receive else mc
        return same(token_rows(y_at(delta), core, j), t3, (j, delta % NY), {"core": 1 - mc})

    def tokens_in(j):
        tok_x(j).wait_recv()
        for d in (0, 1):
            tok_y(j, d, 0, 0).start()
        tok_core(j, 0, False).start()

    def tokens_hop(j):
        for d in (0, 1):
            tok_y(j, d, 0, 1).wait_recv()
        tok_y(j, j % 2, 1, 0).start()
        for delta in (1, -1):
            tok_core(j, delta, False).start()

    def tokens_last(j):
        tok_y(j, j % 2, 1, 1).wait_recv()
        tok_core(j, 2, False).start()

    def tokens_end():
        for j in range(SUBS):
            for delta in (0, 1, -1, 2):
                tok_core(j, delta, True).wait_recv()

    token_plan = {
        2: [(tokens_in, 0)], 3: [(tokens_in, 1)],
        4: [(tokens_in, 2), (tokens_hop, 0)], 5: [(tokens_in, 3), (tokens_hop, 1)],
        6: [(tokens_in, 4), (tokens_last, 0), (tokens_hop, 2)],
        7: [(tokens_in, 5), (tokens_last, 1), (tokens_hop, 3)],
        8: [(tokens_last, 2), (tokens_hop, 4)], 9: [(tokens_last, 3), (tokens_hop, 5)],
        10: [(tokens_last, 4)], 11: [(tokens_last, 5)],
    }
    token_sends = {0: (0, 1, 2), 1: (3, 4), 2: (5,)}
    lags = (2, 1, 0)

    def arrivals(step):
        return {0: (0,), 1: (1, 2), 2: (3, 4), 3: (5, 6), 4: (7,)}.get(step, ())

    def events(u, s):
        lag = lags[u]
        if s == 0:
            send(px_partner, u, mx)
            send(px_mate, u, mx)
        if 1 <= s <= 4:
            for d in (0, 1):
                qz_mine(u, d, s - 1, 1).wait_recv()
                qz_other(u, d, s - 1, 1).wait_recv()
        if s <= 3:
            for d in (0, 1):
                send(qz_mine, u, d, s, 0)
                send(qz_other, u, d, s, 0)
        for i in arrivals(s):
            send(qx_partner, u, i, mx)
            send(qx_mate, u, i, mx)
        if s == 1:
            px_partner(u, partner).wait_recv()
            send(px_forward, u, partner)
        for k in (0, 1):
            hop = s - 1 - k
            if hop == 0:
                if k == 0:
                    px_mate(u, mate).wait_recv()
                else:
                    px_forward(u, across).wait_recv()
            for d in (0, 1):
                if 1 <= hop <= 3 or (hop == 4 and k == d):
                    pzc(u, d, hop - 1, k, 1).wait_recv()
                if 0 <= hop <= 2 or (hop == 3 and k == d):
                    send(pzc, u, d, hop, k, 0)
        for i in arrivals(s - 2 - lag):
            qx_partner(u, i, partner).wait_recv()
            send(qx_forward, u, i, partner)

    def arrived(u, group_at):
        for i in arrivals(group_at):
            qx_mate(u, i, mate).wait_recv()
            qx_forward(u, i, across).wait_recv()

    def product(u, slot, block):
        columns = pl.ds(pl.multiple_of(block * (DM // NZ), DH), DM // NZ)
        return jnp.dot(
            tokv[slot, :, columns], wbuf[u, block].reshape(DM // NZ, WID),
            preferred_element_type=jnp.float32,
        )

    def project(u, slots, shift, group_at):
        if group_at == 0:
            for slot in slots:
                acc[slot + shift] = product(u, slot, mz)
            return
        sides = len(arrivals(group_at))

        def step(index, carry):
            slot = index // sides if len(slots) == 2 else slots[0]
            sign = 1 - 2 * lax.rem(index, sides)
            acc[slot + shift] += product(u, slot, lax.rem(mz + sign * group_at + NZ, NZ))
            return carry

        lax.fori_loop(0, sides * len(slots), step, 0)

    def project_all(u, slot, shift):
        acc[slot + shift] = product(u, slot, 0)

        def step(block, carry):
            acc[slot + shift] += product(u, slot, block)
            return carry

        lax.fori_loop(1, NZ, step, 0)

    def activate(u, slot, shift):
        total = acc[slot + shift]
        act = (total / (1.0 + jnp.exp(-total))).astype(jnp.bfloat16)
        qkv[u, slot] = act
        if u < 2:
            position = lax.broadcasted_iota(jnp.int32, (TOK, DH), 0) + bases[slot]
            last = start_of(bases[slot] + TOK - 1, ends)
            keys = act[:, :DH]
            kept = jnp.where(position >= last, keys, jnp.zeros_like(keys))
            tails[u, slot] = lax.dot_general(
                kept, act[:, DH:], (((0,), (0,)), ((), ())),
                preferred_element_type=jnp.float32,
            )

    def tail_copy(slot, place):
        source = tails.at[1 - mine, slot]
        return copy(source, t4.at[place], ta, (slot,), to_mate)

    def relay(s):
        if s == 0:
            return copy(rt.at[0], rt.at[1], rl, (0,), {"z": z_at(1)})
        return copy(rt.at[2], rt.at[2 + s], rl, (s,), {"z": z_at(1 if s == 1 else 3)})

    def inc_copy(slot, receive):
        place = (mate, across)[slot]
        head = 1 - mine if receive else mine
        return copy(inc_send.at[place], inc.at[head, slot], ia, (slot,), to_mate)

    def square_copy(side, k):
        return copy(
            sends.at[side], sums.at[side * PEERS + k], sq, (side, k), peer(side, k)
        )

    def out_copy(i):
        rows = pl.ds(i * TILE, TILE)
        return copy(osend.at[rows, :], orecv.at[rows, :], oe, (i,), to_partner)

    def row_tail():
        tail_copy(0, mate).wait_recv()
        tail_copy(1, across).wait_recv()
        row_last = start_of((mz + 1) * (NX * TOK) - 1, ends)
        total = jnp.zeros((DH, DH), jnp.float32)
        for j in range(NX):
            here = ((mz * NX + j + 1) * TOK - 1 >= row_last).astype(jnp.float32)
            total = total + here * t4[j]
        rt[0] = total

    def row_pair():
        relay(0).wait_recv()
        row_last = start_of((mz + 1) * (NX * TOK) - 1, ends)
        kept = (mz >= 1) & (mz * (NX * TOK) - 1 >= row_last)
        rt[2] = rt[0] + kept.astype(jnp.float32) * rt[1]

    for step in range(STEPS):
        for u in reversed(range(UNITS)):
            if 0 <= step - 4 * u <= 8:
                events(u, step - 4 * u)
        for j in token_sends.get(step, ()):
            tok_x(j).start()
        for action, j in token_plan.get(step, ()):
            action(j)
        if step == 13:
            tail_copy(0, mx).start()
            tail_copy(1, partner).start()
        if step == 14:
            relay(0).start()
        if step == 15:
            relay(1).start()
            relay(2).start()
        if step == 0:
            for slot in (0, 1):
                t = lax.broadcasted_iota(jnp.int32, (TOK, 1), 0) + bases[slot]
                starts[slot] = start_of(t, ends)
        if step == 4:
            tok_copy.wait()
        for u in (0, 1):
            part = step - 4 * u - 3 - lags[u]
            if 0 <= part <= 4:
                arrived(u, part)
                project(u, (0,), u, part)
                if part == 4:
                    activate(u, 0, u)
        if step == 11:
            tokens_end()
            project_all(0, 1, 1)
            activate(0, 1, 1)
        if step == 12:
            project_all(1, 1, -1)
            activate(1, 1, -1)
        parts = {13: (0, 1), 14: (2, 3), 15: (4,)}.get(step, ())
        for part in parts:
            arrived(2, part)
            project(2, (1, 0), 1, part)
        if step == 13:
            for slot, place in ((0, mx), (1, partner)):
                t4[place] = tails[mine, slot]
            row_tail()
        if step == 14:
            row_pair()
    activate(2, 1, 1)
    activate(2, 0, 1)

    def within(j, slot):
        for i in range(TILES):
            rows, width = slice(i * TILE, (i + 1) * TILE), (i + 1) * TILE
            scores = lax.dot_general(
                qkv[2, slot, rows, j * DH:(j + 1) * DH], qkv[j, slot, 0:width, 0:DH],
                (((1,), (1,)), ((), ())), preferred_element_type=jnp.float32,
            )
            t = lax.broadcasted_iota(jnp.int32, (TILE, 1), 0) + (bases[slot] + i * TILE)
            s = lax.broadcasted_iota(jnp.int32, (1, width), 1) + bases[slot]
            keep = (s <= t) & (s >= starts[slot, rows])
            weights = jnp.where(keep, scores, 0.0).astype(jnp.bfloat16)
            mixed[slot, rows, j * DH:(j + 1) * DH] = jnp.dot(
                weights, qkv[j, slot, 0:width, DH:2 * DH], preferred_element_type=jnp.float32
            )

    for slot in (1, 0):
        within(0, slot)
        within(1, slot)
    relay(1).wait_recv()
    relay(2).wait_recv()
    row_first = start_of(mz * (NX * TOK), ends)
    before = jnp.zeros((DH, DH), jnp.float32)
    for d, at in ((1, 3), (3, 4)):
        row = mz - d
        used = (row >= 0) & ((row + 1) * (NX * TOK) - 1 >= row_first)
        before = before + used.astype(jnp.float32) * rt[at]
    for j in range(NX):
        begin = start_of((mz * NX + j) * TOK, ends)
        state = (begin <= mz * (NX * TOK) - 1).astype(jnp.float32) * before
        for i in range(j):
            used = ((mz * NX + i + 1) * TOK - 1 >= begin).astype(jnp.float32)
            state = state + used * t4[i]
        inc_send[j] = state.astype(jnp.bfloat16)
    for slot in (0, 1):
        inc_copy(slot, False).start()
    for slot, place in ((0, mx), (1, partner)):
        inc[mine, slot] = inc_send[place]
    for slot in (0, 1):
        inc_copy(slot, True).wait_recv()

    def finish_tile(slot, i):
        rows = slice(i * TILE, (i + 1) * TILE)
        carried_on = (starts[slot, rows] <= bases[slot]).astype(jnp.float32)
        squares = jnp.zeros((TILE, DH), jnp.float32)
        for j in (0, 1):
            columns = slice(j * DH, (j + 1) * DH)
            carried = jnp.dot(
                qkv[2, slot, rows, columns], inc[j, slot], preferred_element_type=jnp.float32
            )
            value = mixed[slot, rows, columns] + carried * carried_on
            if slot == 0:
                mixed[slot, rows, columns] = value
            else:
                osend[rows, columns] = value.astype(jnp.bfloat16)
            squares = squares + value * value
        for a in range(TILE // DH):
            flipped = squares[a * DH:(a + 1) * DH, :].T
            row = i * (TILE // DH) + a
            sends[slot, row:row + 1, :] = jnp.sum(flipped, axis=0, keepdims=True)

    for slot in (0, 1):
        sends[slot, TOK // DH:8, :] = jnp.zeros((8 - TOK // DH, DH), jnp.float32)
    for i in range(TILES):
        finish_tile(1, i)
        if i:
            out_copy(i - 1).start()
    for k in range(PEERS):
        square_copy(1, k).start()
    out_copy(TILES - 1).start()
    for i in range(TILES):
        finish_tile(0, i)
    for k in range(1, PEERS):
        square_copy(0, k).start()
    gain = gain_ref[...].astype(jnp.float32)
    is_first = (group == 0).astype(jnp.float32)

    def gain_of(first):
        rows = [gain[j:j + 1] * first + gain[2 + j:3 + j] * (1.0 - first) for j in (0, 1)]
        return jnp.concatenate(rows, axis=1)

    own_gain, other_gain = gain_of(is_first), gain_of(1.0 - is_first)
    own_columns = pl.ds(pl.multiple_of(group * WID, WID), WID)
    other_columns = pl.ds(pl.multiple_of((1 - group) * WID, WID), WID)
    for side in (0, 1):
        for k in range(PEERS):
            if side or k:
                square_copy(side, k).wait_recv()
    total = sends[0]
    for index in range(1, 2 * PEERS):
        total = total + sums[index]
    inverse = lax.rsqrt(total / (PEERS * 4 * DH) + 1e-06)
    scales = [
        jnp.broadcast_to(inverse[a:a + 1, :], (DH, DH)).T for a in range(TOK // DH)
    ]

    def write(columns, source, factor, a):
        rows = slice(a * DH, (a + 1) * DH)
        value = source[rows, :].astype(jnp.float32)
        value = jnp.concatenate(
            [value[:, :DH] * scales[a], value[:, DH:] * scales[a]], axis=1
        )
        out_ref[rows, columns] = (value * factor).astype(jnp.bfloat16)

    for a in range(TOK // DH):
        write(own_columns, mixed.at[0], own_gain, a)
    for i in range(TILES):
        out_copy(i).wait_recv()
        for a in (2 * i, 2 * i + 1):
            write(other_columns, orecv, other_gain, a)

    last = UNITS - 1
    px_mate(last, mx).wait_send()
    px_partner(last, mx).wait_send()
    px_forward(last, partner).wait_send()
    for d in (0, 1):
        for s in range(4):
            qz_mine(last, d, s, 0).wait_send()
            qz_other(last, d, s, 0).wait_send()
            for k in (0, 1):
                if s < 3 or k == d:
                    pzc(last, d, s, k, 0).wait_send()
    for i in range(NZ):
        qx_mate(last, i, mx).wait_send()
        qx_partner(last, i, mx).wait_send()
        qx_forward(last, i, partner).wait_send()
    for j in range(SUBS):
        tok_x(j).wait_send()
        for d in (0, 1):
            tok_y(j, d, 0, 0).wait_send()
        tok_y(j, j % 2, 1, 0).wait_send()
        for delta in (0, 1, -1, 2):
            tok_core(j, delta, False).wait_send()
    for slot in (0, 1):
        tail_copy(slot, mx).wait_send()
        inc_copy(slot, False).wait_send()
    for s in range(3):
        relay(s).wait_send()
    for i in range(TILES):
        out_copy(i).wait_send()
    for side in (0, 1):
        for k in range(PEERS):
            if side or k:
                square_copy(side, k).wait_send()


def shards(tokens, w_query, w_keyval, doc_lengths, norm_gain):
    w_kv = jnp.transpose(w_keyval, (1, 0, 2))
    w_q = jnp.transpose(w_query, (1, 0, 2))
    vmem = pl.BlockSpec(memory_space=pltpu.VMEM)
    smem = pl.BlockSpec(memory_space=pltpu.SMEM)
    anywhere = pl.BlockSpec(memory_space=pl.ANY)

    def dma(*shape):
        return pltpu.SemaphoreType.DMA((2, *shape))

    def units(*shape):
        return pltpu.SemaphoreType.DMA((1 + UNITS, *shape))

    f32, bf16 = jnp.float32, jnp.bfloat16
    return pl.pallas_call(
        kernel,
        out_shape=jax.ShapeDtypeStruct((TOK, 2 * WID), bf16),
        in_specs=[smem, anywhere, anywhere, anywhere, vmem],
        out_specs=vmem,
        scratch_shapes=[
            pltpu.VMEM((UNITS, NZ, NX, ROWS, WID), bf16),
            pltpu.VMEM((UNITS, NZ, QR, WID), bf16),
            pltpu.VMEM((UNITS, PR, WID), bf16),
            pltpu.VMEM((2, TOK, DM), bf16),
            pltpu.VMEM((3, TOK, WID), f32),
            pltpu.VMEM((UNITS, 2, TOK, WID), bf16),
            pltpu.VMEM((2, TOK, 1), jnp.int32),
            pltpu.VMEM((2, 2, DH, DH), f32),
            pltpu.VMEM((NX, DH, DH), f32),
            pltpu.VMEM((5, DH, DH), f32),
            pltpu.VMEM((NX, DH, DH), bf16),
            pltpu.VMEM((2, 2, DH, DH), bf16),
            pltpu.VMEM((2, TOK, WID), f32),
            pltpu.VMEM((2 * PEERS, 8, DH), f32),
            pltpu.VMEM((2, 8, DH), f32),
            pltpu.VMEM((TOK, WID), bf16),
            pltpu.VMEM((TOK, WID), bf16),
            pltpu.SemaphoreType.DMA((10,)),
            units(), units(), units(),
            units(2, 4), units(2, 4), units(2, 4, 2),
            units(NZ), units(NZ), units(NZ),
            dma(SUBS), dma(SUBS, 3), dma(SUBS, NY),
            dma(2), dma(3), dma(2), dma(2, PEERS), dma(TILES),
        ],
        compiler_params=pltpu.CompilerParams(
            collective_id=0, has_side_effects=True, vmem_limit_bytes=62 << 20
        ),
        name="layer",
    )(doc_lengths, tokens, w_kv, w_q, norm_gain.reshape(4, DH))


def solution(mesh):
    grid = Mesh(mesh.devices.reshape(NZ, NX, NY, NC), ("z", "x", "y", "core"))
    seq, fsdp = ("z", "x"), ("y", "core")
    return jax.shard_map(
        shards,
        mesh=grid,
        in_specs=(P(seq, None), P(seq, fsdp, None), P(seq, fsdp, None), P(), P(fsdp)),
        out_specs=P(seq, fsdp),
        check_vma=False,
    )
```

```python
import jax
import jax.numpy as jnp
from jax import lax
from jax.experimental import pallas as pl
from jax.experimental.pallas import tpu as pltpu
from jax.sharding import Mesh, PartitionSpec as P

NZ, NX, NY, NC = 8, 4, 4, 2
PEERS = NY * NC
UNITS = 3
ROWS = 192
PR = 80
QR = ROWS - PR
WID = 256
TOK = 768
DM = 6144
DH = 128
PIECE = TOK // PEERS
SUBS = 3
SUB = PIECE // SUBS
TILE = 256
TILES = TOK // TILE
MESH = pl.DeviceIdType.MESH


def doc_ends(len_ref):
    ends, total = [], jnp.int32(0)
    for i in range(8):
        total = total + len_ref[i]
        ends.append(total)
    return ends


def start_of(position, ends):
    start = jnp.zeros_like(position)
    for end in ends:
        start = jnp.maximum(start, jnp.where(position >= end, end, 0))
    return start


def kernel(
    len_ref, tok_hbm, wkv_hbm, wq_hbm, gain_ref, out_ref,
    wbuf, tbuf, tpb, tokv, acc, qkv, starts, tails, t4, rt, inc_send, inc,
    mixed, sums, sends, osend, orecv, local_sem,
    pxm, pxp, pxf, qzm, qzt, pz, qxm, qxp, qxf, t1, t2, t3,
    ta, rl, ia, sq, oe,
):
    mz, mx = lax.axis_index("z"), lax.axis_index("x")
    my, mc = lax.axis_index("y"), lax.axis_index("core")
    me = my * NC + mc
    mate = mx + 1 - 2 * lax.rem(mx, 2)
    partner = NX - 1 - mx
    across = NX - 1 - mate
    group = mx // 2
    mine = lax.rem(mx, 2)
    ends = doc_ends(len_ref)
    blocks = (mz * NX + mx, mz * NX + partner)
    bases = (blocks[0] * TOK, blocks[1] * TOK)

    def staged(index, source, target):
        return pltpu.make_async_copy(source, target, local_sem.at[index])

    kv_mine = wkv_hbm.at[pl.ds(2 * group, 2)]
    kv_other = wkv_hbm.at[pl.ds(2 * (1 - group), 2)]
    stage = [
        staged(0, kv_mine, wbuf.at[pl.ds(0, 2), mz, mx]),
        staged(1, kv_other.at[:, pl.ds(PR, QR), :], tbuf.at[pl.ds(0, 2), mz]),
        staged(2, kv_other.at[:, pl.ds(0, PR), :], tpb.at[pl.ds(0, 2)]),
    ]
    for j in (0, 1):
        columns = pl.ds(j * DH, DH)
        q_mine, q_other = wq_hbm.at[2 * group + j], wq_hbm.at[2 * (1 - group) + j]
        stage += [
            staged(4 + 3 * j, q_mine, wbuf.at[2, mz, mx, :, columns]),
            staged(5 + 3 * j, q_other.at[pl.ds(PR, QR), :], tbuf.at[2, mz, :, columns]),
            staged(6 + 3 * j, q_other.at[pl.ds(0, PR), :], tpb.at[2, :, columns]),
        ]
    for item in stage:
        item.start()
    tok_copy = pltpu.make_async_copy(tok_hbm, tokv.at[0], local_sem.at[3])
    tok_copy.start()

    def z_at(delta):
        return lax.rem(mz + delta + NZ, NZ)

    def y_at(delta):
        return lax.rem(my + delta + NY, NY)

    def peer(side, k):
        index = lax.rem(me + k, PEERS)
        return {
            "x": mx if side == 0 else partner,
            "y": index // NC,
            "core": lax.rem(index, NC),
        }

    barrier = pltpu.get_barrier_semaphore()

    def greet(target):
        pl.semaphore_signal(barrier, inc=1, device_id=target, device_id_type=MESH)

    greet({"x": mate})
    for delta in (1, -1, 3, -3):
        greet({"z": z_at(delta)})
    for k in range(PEERS):
        if k:
            greet(peer(0, k))
        greet(peer(1, k))
    pl.semaphore_wait(barrier, 5 + 2 * PEERS - 1)
    for item in stage:
        item.wait()

    def copy(src, dst, sems, index, target):
        return pltpu.make_async_remote_copy(
            src_ref=src, dst_ref=dst, send_sem=sems.at[(0, *index)],
            recv_sem=sems.at[(1, *index)], device_id=target, device_id_type=MESH,
        )

    def same(ref, sems, index, target):
        return copy(ref, ref, sems, index, target)

    def unit_copy(src, dst, sems, u, rest, target):
        return pltpu.make_async_remote_copy(
            src_ref=src, dst_ref=dst, send_sem=sems.at[(0, *rest)],
            recv_sem=sems.at[(1 + u, *rest)], device_id=target, device_id_type=MESH,
        )

    def unit_same(ref, sems, u, rest, target):
        return unit_copy(ref, ref, sems, u, rest, target)

    def send(make, u, *args):
        if u:
            make(u - 1, *args).wait_send()
        make(u, *args).start()

    to_mate, to_partner = {"x": mate}, {"x": partner}

    def upper(u, x):
        return wbuf.at[u, mz, x, pl.ds(0, PR), :]

    def px_mate(u, x):
        return unit_same(upper(u, x), pxm, u, (), to_mate)

    def px_partner(u, x):
        return unit_copy(tpb.at[u], upper(u, x), pxp, u, (), to_partner)

    def px_forward(u, x):
        return unit_same(upper(u, x), pxf, u, (), to_mate)

    def qz_part(d, s, lag):
        sign = 1 - 2 * d
        lo, size = (0, QR) if s < 3 else ((0, 48) if d == 0 else (48, QR - 48))
        return z_at(-sign * (s + lag)), lo, size, {"z": z_at(sign)}

    def qz_mine(u, d, s, lag):
        block, lo, size, target = qz_part(d, s, lag)
        return unit_same(wbuf.at[u, block, mx, pl.ds(PR + lo, size), :], qzm, u, (d, s), target)

    def qz_other(u, d, s, lag):
        block, lo, size, target = qz_part(d, s, lag)
        return unit_same(tbuf.at[u, block, pl.ds(lo, size), :], qzt, u, (d, s), target)

    def pzc(u, d, s, k, lag):
        sign = 1 - 2 * d
        block = z_at(-sign * (s + lag))
        pair = group if k == 0 else 1 - group
        return unit_same(
            wbuf.at[u, block, pl.ds(2 * pair, 2), pl.ds(0, PR), :],
            pz, u, (d, s, k), {"z": z_at(sign)},
        )

    def lower(u, k, x):
        return wbuf.at[u, pl.ds(2 * k, 2), x, pl.ds(PR, QR), :]

    def qx_mate(u, k, x):
        return unit_same(lower(u, k, x), qxm, u, (k,), to_mate)

    def qx_partner(u, k, x):
        return unit_copy(
            tbuf.at[u, pl.ds(2 * k, 2)], lower(u, k, x), qxp, u, (k,), to_partner
        )

    def qx_forward(u, k, x):
        return unit_same(lower(u, k, x), qxf, u, (k,), to_mate)

    def token_rows(y, core, j, half=None):
        start = (y * NC + core) * PIECE + j * SUB
        if half is None:
            return tokv.at[1, pl.ds(start, SUB), :]
        return tokv.at[1, pl.ds(start + half * (SUB // 2), SUB // 2), :]

    def tok_x(j):
        start = me * PIECE + j * SUB
        return copy(tok_hbm.at[pl.ds(start, SUB), :], token_rows(my, mc, j), t1, (j,), to_partner)

    def tok_y(j, d, s, lag):
        sign = 1 - 2 * d
        rows = token_rows(y_at(-sign * (s + lag)), mc, j, None if s == 0 else d)
        return same(rows, t2, (j, d, s), {"y": y_at(sign)})

    def tok_core(j, delta, receive):
        core = 1 - mc if receive else mc
        return same(token_rows(y_at(delta), core, j), t3, (j, delta % NY), {"core": 1 - mc})

    def tokens_in(j):
        tok_x(j).wait_recv()
        for d in (0, 1):
            tok_y(j, d, 0, 0).start()
        tok_core(j, 0, False).start()

    def tokens_hop(j):
        for d in (0, 1):
            tok_y(j, d, 0, 1).wait_recv()
            tok_y(j, d, 1, 0).start()
        for delta in (1, -1):
            tok_core(j, delta, False).start()

    def tokens_last(j):
        for d in (0, 1):
            tok_y(j, d, 1, 1).wait_recv()
        tok_core(j, 2, False).start()

    def tokens_end():
        for j in range(SUBS):
            for delta in (0, 1, -1, 2):
                tok_core(j, delta, True).wait_recv()

    token_plan = {
        3: [(tokens_in, 0)], 5: [(tokens_in, 1)], 6: [(tokens_hop, 0)],
        7: [(tokens_hop, 1)], 8: [(tokens_in, 2), (tokens_last, 0)], 9: [(tokens_last, 1)],
        11: [(tokens_hop, 2)], 12: [(tokens_last, 2)],
    }

    def phase1_start(n):
        for d in (0, 1):
            send(qz_mine, n, d, 0, 0)
            send(qz_other, n, d, 0, 0)
        send(px_partner, n, mx)
        send(px_mate, n, mx)

    def phase1_step(n, s):
        for d in (0, 1):
            qz_mine(n, d, s - 1, 1).wait_recv()
            qz_other(n, d, s - 1, 1).wait_recv()
            send(qz_mine, n, d, s, 0)
            send(qz_other, n, d, s, 0)
        if s == 1:
            px_partner(n, partner).wait_recv()
            send(px_forward, n, partner)

    def phase2_start(p):
        px_mate(p, mate).wait_recv()
        px_forward(p, across).wait_recv()
        for k in (0, 1):
            for d in (0, 1):
                send(pzc, p, d, 0, k, 0)
        for d in (0, 1):
            qz_mine(p, d, 3, 1).wait_recv()
            qz_other(p, d, 3, 1).wait_recv()
        for k in range(4):
            send(qx_partner, p, k, mx)
            send(qx_mate, p, k, mx)

    def phase2_step(p, s):
        for k in (0, 1):
            for d in (0, 1):
                pzc(p, d, s - 1, k, 1).wait_recv()
                if s < 3 or k == d:
                    send(pzc, p, d, s, k, 0)
        for k in ((0,), (1, 2), (3,))[s - 1]:
            qx_partner(p, k, partner).wait_recv()
            send(qx_forward, p, k, partner)

    def phase2_end(p):
        for d in (0, 1):
            pzc(p, d, 3, d, 1).wait_recv()
        for k in range(4):
            qx_mate(p, k, mate).wait_recv()
            qx_forward(p, k, across).wait_recv()

    def project(u, slot, lo, hi):
        if lo == 0:
            acc[...] = jnp.zeros_like(acc)

        def step(pair, carry):
            columns = pl.ds(pl.multiple_of(pair * (DM // 4), 128), DM // 4)
            acc[...] += jnp.dot(
                tokv[slot, :, columns],
                wbuf[u, pl.ds(2 * pair, 2)].reshape(DM // 4, WID),
                preferred_element_type=jnp.float32,
            )
            return carry

        lax.fori_loop(lo, hi, step, 0)

    def activate(u, slot):
        total = acc[...]
        act = (total / (1.0 + jnp.exp(-total))).astype(jnp.bfloat16)
        qkv[u, slot] = act
        if u < 2:
            position = lax.broadcasted_iota(jnp.int32, (TOK, DH), 0) + bases[slot]
            last = start_of(bases[slot] + TOK - 1, ends)
            keys = act[:, :DH]
            kept = jnp.where(position >= last, keys, jnp.zeros_like(keys))
            tails[u, slot] = lax.dot_general(
                kept, act[:, DH:], (((0,), (0,)), ((), ())),
                preferred_element_type=jnp.float32,
            )

    def tail_copy(slot, place):
        source = tails.at[1 - mine, slot]
        return copy(source, t4.at[place], ta, (slot,), to_mate)

    def relay(s):
        if s == 0:
            return copy(rt.at[0], rt.at[1], rl, (0,), {"z": z_at(1)})
        return copy(rt.at[2], rt.at[2 + s], rl, (s,), {"z": z_at(1 if s == 1 else 3)})

    def inc_copy(slot, receive):
        place = (mate, across)[slot]
        head = 1 - mine if receive else mine
        return copy(inc_send.at[place], inc.at[head, slot], ia, (slot,), to_mate)

    def square_copy(side, k):
        return copy(
            sends.at[side], sums.at[side * PEERS + k], sq, (side, k), peer(side, k)
        )

    def out_copy(i):
        rows = pl.ds(i * TILE, TILE)
        return copy(osend.at[rows, :], orecv.at[rows, :], oe, (i,), to_partner)

    def row_tail():
        tail_copy(0, mate).wait_recv()
        tail_copy(1, across).wait_recv()
        row_last = start_of((mz + 1) * (NX * TOK) - 1, ends)
        total = jnp.zeros((DH, DH), jnp.float32)
        for j in range(NX):
            here = ((mz * NX + j + 1) * TOK - 1 >= row_last).astype(jnp.float32)
            total = total + here * t4[j]
        rt[0] = total

    def row_pair():
        relay(0).wait_recv()
        row_last = start_of((mz + 1) * (NX * TOK) - 1, ends)
        kept = (mz >= 1) & (mz * (NX * TOK) - 1 >= row_last)
        rt[2] = rt[0] + kept.astype(jnp.float32) * rt[1]

    for step in range(16):
        r, s = step // 4, step % 4
        n, p, c = r, r - 1, r - 2
        if s == 0:
            if n < UNITS:
                phase1_start(n)
            if r == 0:
                tok_x(0).start()
                tok_x(1).start()
                for slot in (0, 1):
                    t = lax.broadcasted_iota(jnp.int32, (TOK, 1), 0) + bases[slot]
                    starts[slot] = start_of(t, ends)
            if p >= 0:
                phase2_start(p)
            if r == 1:
                tok_x(2).start()
            if c >= 0:
                phase2_end(c)
        else:
            if n < UNITS:
                phase1_step(n, s)
            if p >= 0:
                phase2_step(p, s)
        for action, j in token_plan.get(step, ()):
            action(j)
        if r == 2:
            if s == 0:
                tok_copy.wait()
            project(0, 0, s, s + 1)
            if s == 3:
                activate(0, 0)
        if step == 12:
            project(1, 0, 0, 4)
            activate(1, 0)
        if step == 13:
            tokens_end()
            project(0, 1, 0, 4)
            activate(0, 1)
        if step == 14:
            project(1, 1, 0, 4)
            activate(1, 1)
        if step == 15:
            tail_copy(0, mx).start()
            tail_copy(1, partner).start()
            for slot, place in ((0, mx), (1, partner)):
                t4[place] = tails[mine, slot]

    def within(j, slot):
        for i in range(TILES):
            rows, width = slice(i * TILE, (i + 1) * TILE), (i + 1) * TILE
            scores = lax.dot_general(
                qkv[2, slot, rows, j * DH:(j + 1) * DH], qkv[j, slot, 0:width, 0:DH],
                (((1,), (1,)), ((), ())), preferred_element_type=jnp.float32,
            )
            t = lax.broadcasted_iota(jnp.int32, (TILE, 1), 0) + (bases[slot] + i * TILE)
            s = lax.broadcasted_iota(jnp.int32, (1, width), 1) + bases[slot]
            keep = (s <= t) & (s >= starts[slot, rows])
            weights = jnp.where(keep, scores, 0.0).astype(jnp.bfloat16)
            mixed[slot, rows, j * DH:(j + 1) * DH] = jnp.dot(
                weights, qkv[j, slot, 0:width, DH:2 * DH], preferred_element_type=jnp.float32
            )

    phase2_end(2)
    row_tail()
    project(2, 1, 0, 2)
    relay(0).start()
    project(2, 1, 2, 4)
    activate(2, 1)
    project(2, 0, 0, 2)
    row_pair()
    project(2, 0, 2, 4)
    relay(1).start()
    relay(2).start()
    activate(2, 0)
    for slot in (1, 0):
        within(0, slot)
        within(1, slot)
    relay(1).wait_recv()
    relay(2).wait_recv()
    row_first = start_of(mz * (NX * TOK), ends)
    before = jnp.zeros((DH, DH), jnp.float32)
    for d, at in ((1, 3), (3, 4)):
        row = mz - d
        used = (row >= 0) & ((row + 1) * (NX * TOK) - 1 >= row_first)
        before = before + used.astype(jnp.float32) * rt[at]
    for j in range(NX):
        begin = start_of((mz * NX + j) * TOK, ends)
        state = (begin <= mz * (NX * TOK) - 1).astype(jnp.float32) * before
        for i in range(j):
            used = ((mz * NX + i + 1) * TOK - 1 >= begin).astype(jnp.float32)
            state = state + used * t4[i]
        inc_send[j] = state.astype(jnp.bfloat16)
    for slot in (0, 1):
        inc_copy(slot, False).start()
    for slot, place in ((0, mx), (1, partner)):
        inc[mine, slot] = inc_send[place]
    for slot in (0, 1):
        inc_copy(slot, True).wait_recv()

    def finish_tile(slot, i):
        rows = slice(i * TILE, (i + 1) * TILE)
        carried_on = (starts[slot, rows] <= bases[slot]).astype(jnp.float32)
        squares = jnp.zeros((TILE, DH), jnp.float32)
        for j in (0, 1):
            columns = slice(j * DH, (j + 1) * DH)
            carried = jnp.dot(
                qkv[2, slot, rows, columns], inc[j, slot], preferred_element_type=jnp.float32
            )
            value = mixed[slot, rows, columns] + carried * carried_on
            if slot == 0:
                mixed[slot, rows, columns] = value
            else:
                osend[rows, columns] = value.astype(jnp.bfloat16)
            squares = squares + value * value
        for a in range(TILE // DH):
            flipped = squares[a * DH:(a + 1) * DH, :].T
            row = i * (TILE // DH) + a
            sends[slot, row:row + 1, :] = jnp.sum(flipped, axis=0, keepdims=True)

    for slot in (0, 1):
        sends[slot, TOK // DH:8, :] = jnp.zeros((8 - TOK // DH, DH), jnp.float32)
    for i in range(TILES):
        finish_tile(1, i)
        if i:
            out_copy(i - 1).start()
    for k in range(PEERS):
        square_copy(1, k).start()
    out_copy(TILES - 1).start()
    for i in range(TILES):
        finish_tile(0, i)
    for k in range(1, PEERS):
        square_copy(0, k).start()
    gain = gain_ref[...].astype(jnp.float32)
    is_first = (group == 0).astype(jnp.float32)

    def gain_of(first):
        rows = [gain[j:j + 1] * first + gain[2 + j:3 + j] * (1.0 - first) for j in (0, 1)]
        return jnp.concatenate(rows, axis=1)

    own_gain, other_gain = gain_of(is_first), gain_of(1.0 - is_first)
    own_columns = pl.ds(pl.multiple_of(group * WID, WID), WID)
    other_columns = pl.ds(pl.multiple_of((1 - group) * WID, WID), WID)
    for side in (0, 1):
        for k in range(PEERS):
            if side or k:
                square_copy(side, k).wait_recv()
    total = sends[0]
    for index in range(1, 2 * PEERS):
        total = total + sums[index]
    inverse = lax.rsqrt(total / (PEERS * 4 * DH) + 1e-06)
    scales = [
        jnp.broadcast_to(inverse[a:a + 1, :], (DH, DH)).T for a in range(TOK // DH)
    ]

    def write(columns, source, factor, a):
        rows = slice(a * DH, (a + 1) * DH)
        value = source[rows, :].astype(jnp.float32)
        value = jnp.concatenate(
            [value[:, :DH] * scales[a], value[:, DH:] * scales[a]], axis=1
        )
        out_ref[rows, columns] = (value * factor).astype(jnp.bfloat16)

    for a in range(TOK // DH):
        write(own_columns, mixed.at[0], own_gain, a)
    for i in range(TILES):
        out_copy(i).wait_recv()
        for a in (2 * i, 2 * i + 1):
            write(other_columns, orecv, other_gain, a)

    last = UNITS - 1
    px_mate(last, mx).wait_send()
    px_partner(last, mx).wait_send()
    px_forward(last, partner).wait_send()
    for d in (0, 1):
        for s in range(4):
            qz_mine(last, d, s, 0).wait_send()
            qz_other(last, d, s, 0).wait_send()
            for k in (0, 1):
                if s < 3 or k == d:
                    pzc(last, d, s, k, 0).wait_send()
    for k in range(4):
        qx_mate(last, k, mx).wait_send()
        qx_partner(last, k, mx).wait_send()
        qx_forward(last, k, partner).wait_send()
    for j in range(SUBS):
        tok_x(j).wait_send()
        for d in (0, 1):
            tok_y(j, d, 0, 0).wait_send()
            tok_y(j, d, 1, 0).wait_send()
        for delta in (0, 1, -1, 2):
            tok_core(j, delta, False).wait_send()
    for slot in (0, 1):
        tail_copy(slot, mx).wait_send()
        inc_copy(slot, False).wait_send()
    for s in range(3):
        relay(s).wait_send()
    for i in range(TILES):
        out_copy(i).wait_send()
    for side in (0, 1):
        for k in range(PEERS):
            if side or k:
                square_copy(side, k).wait_send()


def shards(tokens, w_query, w_keyval, doc_lengths, norm_gain):
    w_kv = jnp.transpose(w_keyval, (1, 0, 2))
    w_q = jnp.transpose(w_query, (1, 0, 2))
    vmem = pl.BlockSpec(memory_space=pltpu.VMEM)
    smem = pl.BlockSpec(memory_space=pltpu.SMEM)
    anywhere = pl.BlockSpec(memory_space=pl.ANY)

    def dma(*shape):
        return pltpu.SemaphoreType.DMA((2, *shape))

    def units(*shape):
        return pltpu.SemaphoreType.DMA((1 + UNITS, *shape))

    f32, bf16 = jnp.float32, jnp.bfloat16
    return pl.pallas_call(
        kernel,
        out_shape=jax.ShapeDtypeStruct((TOK, 2 * WID), bf16),
        in_specs=[smem, anywhere, anywhere, anywhere, vmem],
        out_specs=vmem,
        scratch_shapes=[
            pltpu.VMEM((UNITS, NZ, NX, ROWS, WID), bf16),
            pltpu.VMEM((UNITS, NZ, QR, WID), bf16),
            pltpu.VMEM((UNITS, PR, WID), bf16),
            pltpu.VMEM((2, TOK, DM), bf16),
            pltpu.VMEM((TOK, WID), f32),
            pltpu.VMEM((UNITS, 2, TOK, WID), bf16),
            pltpu.VMEM((2, TOK, 1), jnp.int32),
            pltpu.VMEM((2, 2, DH, DH), f32),
            pltpu.VMEM((NX, DH, DH), f32),
            pltpu.VMEM((5, DH, DH), f32),
            pltpu.VMEM((NX, DH, DH), bf16),
            pltpu.VMEM((2, 2, DH, DH), bf16),
            pltpu.VMEM((2, TOK, WID), f32),
            pltpu.VMEM((2 * PEERS, 8, DH), f32),
            pltpu.VMEM((2, 8, DH), f32),
            pltpu.VMEM((TOK, WID), bf16),
            pltpu.VMEM((TOK, WID), bf16),
            pltpu.SemaphoreType.DMA((10,)),
            units(), units(), units(),
            units(2, 4), units(2, 4), units(2, 4, 2),
            units(4), units(4), units(4),
            dma(SUBS), dma(SUBS, 2, 2), dma(SUBS, NY),
            dma(2), dma(3), dma(2), dma(2, PEERS), dma(TILES),
        ],
        compiler_params=pltpu.CompilerParams(
            collective_id=0, has_side_effects=True, vmem_limit_bytes=62 << 20
        ),
        name="layer",
    )(doc_lengths, tokens, w_kv, w_q, norm_gain.reshape(4, DH))


def solution(mesh):
    grid = Mesh(mesh.devices.reshape(NZ, NX, NY, NC), ("z", "x", "y", "core"))
    seq, fsdp = ("z", "x"), ("y", "core")
    return jax.shard_map(
        shards,
        mesh=grid,
        in_specs=(P(seq, None), P(seq, fsdp, None), P(seq, fsdp, None), P(), P(fsdp)),
        out_specs=P(seq, fsdp),
        check_vma=False,
    )
```

```python
import jax
import jax.numpy as jnp
from jax import lax
from jax.experimental import pallas as pl
from jax.experimental.pallas import tpu as pltpu
from jax.sharding import Mesh, PartitionSpec as P

NZ, NX, NY, NC = 8, 4, 4, 2
PEERS = NY * NC
UNITS = 3
ROWS = 192
PR = 80
QR = ROWS - PR
WID = 256
TOK = 768
DM = 6144
DH = 128
PIECE = TOK // PEERS
SUBS = 3
SUB = PIECE // SUBS
TILE = 256
TILES = TOK // TILE
MESH = pl.DeviceIdType.MESH


def doc_ends(len_ref):
    ends, total = [], jnp.int32(0)
    for i in range(8):
        total = total + len_ref[i]
        ends.append(total)
    return ends


def start_of(position, ends):
    start = jnp.zeros_like(position)
    for end in ends:
        start = jnp.maximum(start, jnp.where(position >= end, end, 0))
    return start


def kernel(
    len_ref, tok_hbm, wkv_hbm, wq_hbm, gain_ref, out_ref,
    wbuf, tbuf, tpb, tokv, acc, qkv, starts, tails, t4, rt, inc_send, inc,
    mixed, sums, sends, osend, orecv, local_sem,
    pxm, pxp, pxf, qzm, qzt, pz, qxm, qxp, qxf, t1, t2, t3,
    ta, rl, ia, sq, oe,
):
    mz, mx = lax.axis_index("z"), lax.axis_index("x")
    my, mc = lax.axis_index("y"), lax.axis_index("core")
    me = my * NC + mc
    mate = mx + 1 - 2 * lax.rem(mx, 2)
    partner = NX - 1 - mx
    across = NX - 1 - mate
    group = mx // 2
    mine = lax.rem(mx, 2)
    ends = doc_ends(len_ref)
    blocks = (mz * NX + mx, mz * NX + partner)
    bases = (blocks[0] * TOK, blocks[1] * TOK)

    def staged(index, source, target):
        return pltpu.make_async_copy(source, target, local_sem.at[index])

    kv_mine = wkv_hbm.at[pl.ds(2 * group, 2)]
    kv_other = wkv_hbm.at[pl.ds(2 * (1 - group), 2)]
    stage = [
        staged(0, kv_mine, wbuf.at[pl.ds(0, 2), mz, mx]),
        staged(1, kv_other.at[:, pl.ds(PR, QR), :], tbuf.at[pl.ds(0, 2), mz]),
        staged(2, kv_other.at[:, pl.ds(0, PR), :], tpb.at[pl.ds(0, 2)]),
    ]
    for j in (0, 1):
        columns = pl.ds(j * DH, DH)
        q_mine, q_other = wq_hbm.at[2 * group + j], wq_hbm.at[2 * (1 - group) + j]
        stage += [
            staged(4 + 3 * j, q_mine, wbuf.at[2, mz, mx, :, columns]),
            staged(5 + 3 * j, q_other.at[pl.ds(PR, QR), :], tbuf.at[2, mz, :, columns]),
            staged(6 + 3 * j, q_other.at[pl.ds(0, PR), :], tpb.at[2, :, columns]),
        ]
    for item in stage:
        item.start()
    tok_copy = pltpu.make_async_copy(tok_hbm, tokv.at[0], local_sem.at[3])
    tok_copy.start()

    def z_at(delta):
        return lax.rem(mz + delta + NZ, NZ)

    def y_at(delta):
        return lax.rem(my + delta + NY, NY)

    def peer(side, k):
        index = lax.rem(me + k, PEERS)
        return {
            "x": mx if side == 0 else partner,
            "y": index // NC,
            "core": lax.rem(index, NC),
        }

    barrier = pltpu.get_barrier_semaphore()

    def greet(target):
        pl.semaphore_signal(barrier, inc=1, device_id=target, device_id_type=MESH)

    greet({"x": mate})
    for delta in (1, -1, 3, -3):
        greet({"z": z_at(delta)})
    for k in range(PEERS):
        if k:
            greet(peer(0, k))
        greet(peer(1, k))
    pl.semaphore_wait(barrier, 5 + 2 * PEERS - 1)
    for item in stage:
        item.wait()

    def copy(src, dst, sems, index, target):
        return pltpu.make_async_remote_copy(
            src_ref=src, dst_ref=dst, send_sem=sems.at[(0, *index)],
            recv_sem=sems.at[(1, *index)], device_id=target, device_id_type=MESH,
        )

    def same(ref, sems, index, target):
        return copy(ref, ref, sems, index, target)

    def unit_copy(src, dst, sems, u, rest, target):
        return pltpu.make_async_remote_copy(
            src_ref=src, dst_ref=dst, send_sem=sems.at[(0, *rest)],
            recv_sem=sems.at[(1 + u, *rest)], device_id=target, device_id_type=MESH,
        )

    def unit_same(ref, sems, u, rest, target):
        return unit_copy(ref, ref, sems, u, rest, target)

    def send(make, u, *args):
        if u:
            make(u - 1, *args).wait_send()
        make(u, *args).start()

    to_mate, to_partner = {"x": mate}, {"x": partner}

    def upper(u, x):
        return wbuf.at[u, mz, x, pl.ds(0, PR), :]

    def px_mate(u, x):
        return unit_same(upper(u, x), pxm, u, (), to_mate)

    def px_partner(u, x):
        return unit_copy(tpb.at[u], upper(u, x), pxp, u, (), to_partner)

    def px_forward(u, x):
        return unit_same(upper(u, x), pxf, u, (), to_mate)

    def qz_part(d, s, lag):
        sign = 1 - 2 * d
        lo, size = (0, QR) if s < 3 else ((0, 48) if d == 0 else (48, QR - 48))
        return z_at(-sign * (s + lag)), lo, size, {"z": z_at(sign)}

    def qz_mine(u, d, s, lag):
        block, lo, size, target = qz_part(d, s, lag)
        return unit_same(wbuf.at[u, block, mx, pl.ds(PR + lo, size), :], qzm, u, (d, s), target)

    def qz_other(u, d, s, lag):
        block, lo, size, target = qz_part(d, s, lag)
        return unit_same(tbuf.at[u, block, pl.ds(lo, size), :], qzt, u, (d, s), target)

    def pzc(u, d, s, k, lag):
        sign = 1 - 2 * d
        block = z_at(-sign * (s + lag))
        pair = group if k == 0 else 1 - group
        return unit_same(
            wbuf.at[u, block, pl.ds(2 * pair, 2), pl.ds(0, PR), :],
            pz, u, (d, s, k), {"z": z_at(sign)},
        )

    def lower(u, k, x):
        return wbuf.at[u, pl.ds(2 * k, 2), x, pl.ds(PR, QR), :]

    def qx_mate(u, k, x):
        return unit_same(lower(u, k, x), qxm, u, (k,), to_mate)

    def qx_partner(u, k, x):
        return unit_copy(
            tbuf.at[u, pl.ds(2 * k, 2)], lower(u, k, x), qxp, u, (k,), to_partner
        )

    def qx_forward(u, k, x):
        return unit_same(lower(u, k, x), qxf, u, (k,), to_mate)

    def token_rows(y, core, j, half=None):
        start = (y * NC + core) * PIECE + j * SUB
        if half is None:
            return tokv.at[1, pl.ds(start, SUB), :]
        return tokv.at[1, pl.ds(start + half * (SUB // 2), SUB // 2), :]

    def tok_x(j):
        start = me * PIECE + j * SUB
        return copy(tok_hbm.at[pl.ds(start, SUB), :], token_rows(my, mc, j), t1, (j,), to_partner)

    def tok_y(j, d, s, lag):
        sign = 1 - 2 * d
        rows = token_rows(y_at(-sign * (s + lag)), mc, j, None if s == 0 else d)
        return same(rows, t2, (j, d, s), {"y": y_at(sign)})

    def tok_core(j, delta, receive):
        core = 1 - mc if receive else mc
        return same(token_rows(y_at(delta), core, j), t3, (j, delta % NY), {"core": 1 - mc})

    def tokens_in(j):
        tok_x(j).wait_recv()
        for d in (0, 1):
            tok_y(j, d, 0, 0).start()
        tok_core(j, 0, False).start()

    def tokens_hop(j):
        for d in (0, 1):
            tok_y(j, d, 0, 1).wait_recv()
            tok_y(j, d, 1, 0).start()
        for delta in (1, -1):
            tok_core(j, delta, False).start()

    def tokens_last(j):
        for d in (0, 1):
            tok_y(j, d, 1, 1).wait_recv()
        tok_core(j, 2, False).start()

    def tokens_end():
        for j in range(SUBS):
            for delta in (0, 1, -1, 2):
                tok_core(j, delta, True).wait_recv()

    token_plan = {
        3: [(tokens_in, 0)], 5: [(tokens_in, 1)], 6: [(tokens_hop, 0)],
        7: [(tokens_hop, 1)], 8: [(tokens_in, 2), (tokens_last, 0)], 9: [(tokens_last, 1)],
        11: [(tokens_hop, 2)], 12: [(tokens_last, 2)],
    }

    def phase1_start(n):
        for d in (0, 1):
            send(qz_mine, n, d, 0, 0)
            send(qz_other, n, d, 0, 0)
        send(px_partner, n, mx)
        send(px_mate, n, mx)

    def phase1_step(n, s):
        for d in (0, 1):
            qz_mine(n, d, s - 1, 1).wait_recv()
            qz_other(n, d, s - 1, 1).wait_recv()
            send(qz_mine, n, d, s, 0)
            send(qz_other, n, d, s, 0)
        if s == 1:
            px_partner(n, partner).wait_recv()
            send(px_forward, n, partner)

    def phase2_start(p):
        px_mate(p, mate).wait_recv()
        px_forward(p, across).wait_recv()
        for k in (0, 1):
            for d in (0, 1):
                send(pzc, p, d, 0, k, 0)
        for d in (0, 1):
            qz_mine(p, d, 3, 1).wait_recv()
            qz_other(p, d, 3, 1).wait_recv()
        for k in range(4):
            send(qx_partner, p, k, mx)
            send(qx_mate, p, k, mx)

    def phase2_step(p, s):
        for k in (0, 1):
            for d in (0, 1):
                pzc(p, d, s - 1, k, 1).wait_recv()
                if s < 3 or k == d:
                    send(pzc, p, d, s, k, 0)
        if p == UNITS - 1 and s == 3:
            tail_copy(0, mx).start()
            tail_copy(1, partner).start()
        for k in ((0,), (1, 2), (3,))[s - 1]:
            qx_partner(p, k, partner).wait_recv()
            send(qx_forward, p, k, partner)

    def phase2_end(p):
        for d in (0, 1):
            pzc(p, d, 3, d, 1).wait_recv()
        for k in range(4):
            qx_mate(p, k, mate).wait_recv()
            qx_forward(p, k, across).wait_recv()

    def project(u, slot, lo, hi):
        if lo == 0:
            acc[slot] = jnp.zeros((TOK, WID), jnp.float32)

        def step(pair, carry):
            columns = pl.ds(pl.multiple_of(pair * (DM // 4), 128), DM // 4)
            acc[slot] += jnp.dot(
                tokv[slot, :, columns],
                wbuf[u, pl.ds(2 * pair, 2)].reshape(DM // 4, WID),
                preferred_element_type=jnp.float32,
            )
            return carry

        lax.fori_loop(lo, hi, step, 0)

    def activate(u, slot):
        total = acc[slot]
        act = (total / (1.0 + jnp.exp(-total))).astype(jnp.bfloat16)
        qkv[u, slot] = act
        if u < 2:
            position = lax.broadcasted_iota(jnp.int32, (TOK, DH), 0) + bases[slot]
            last = start_of(bases[slot] + TOK - 1, ends)
            keys = act[:, :DH]
            kept = jnp.where(position >= last, keys, jnp.zeros_like(keys))
            tails[u, slot] = lax.dot_general(
                kept, act[:, DH:], (((0,), (0,)), ((), ())),
                preferred_element_type=jnp.float32,
            )

    def tail_copy(slot, place):
        source = tails.at[1 - mine, slot]
        return copy(source, t4.at[place], ta, (slot,), to_mate)

    def relay(s):
        if s == 0:
            return copy(rt.at[0], rt.at[1], rl, (0,), {"z": z_at(1)})
        return copy(rt.at[2], rt.at[2 + s], rl, (s,), {"z": z_at(1 if s == 1 else 3)})

    def inc_copy(slot, receive):
        place = (mate, across)[slot]
        head = 1 - mine if receive else mine
        return copy(inc_send.at[place], inc.at[head, slot], ia, (slot,), to_mate)

    def square_copy(side, k):
        return copy(
            sends.at[side], sums.at[side * PEERS + k], sq, (side, k), peer(side, k)
        )

    def out_copy(i):
        rows = pl.ds(i * TILE, TILE)
        return copy(osend.at[rows, :], orecv.at[rows, :], oe, (i,), to_partner)

    def row_tail():
        tail_copy(0, mate).wait_recv()
        tail_copy(1, across).wait_recv()
        row_last = start_of((mz + 1) * (NX * TOK) - 1, ends)
        total = jnp.zeros((DH, DH), jnp.float32)
        for j in range(NX):
            here = ((mz * NX + j + 1) * TOK - 1 >= row_last).astype(jnp.float32)
            total = total + here * t4[j]
        rt[0] = total

    def row_pair():
        relay(0).wait_recv()
        row_last = start_of((mz + 1) * (NX * TOK) - 1, ends)
        kept = (mz >= 1) & (mz * (NX * TOK) - 1 >= row_last)
        rt[2] = rt[0] + kept.astype(jnp.float32) * rt[1]

    for step in range(16):
        r, s = step // 4, step % 4
        n, p, c = r, r - 1, r - 2
        if s == 0:
            if n < UNITS:
                phase1_start(n)
            if r == 0:
                tok_x(0).start()
                tok_x(1).start()
                for slot in (0, 1):
                    t = lax.broadcasted_iota(jnp.int32, (TOK, 1), 0) + bases[slot]
                    starts[slot] = start_of(t, ends)
            if p >= 0:
                phase2_start(p)
            if r == 1:
                tok_x(2).start()
            if c >= 0:
                phase2_end(c)
        else:
            if n < UNITS:
                phase1_step(n, s)
            if p >= 0:
                phase2_step(p, s)
        for action, j in token_plan.get(step, ()):
            action(j)
        if r == 2:
            if s == 0:
                tok_copy.wait()
            project(0, 0, s, s + 1)
            if s == 3:
                activate(0, 0)
        if step == 12:
            project(1, 0, 0, 4)
            activate(1, 0)
        if step == 13:
            tokens_end()
            project(0, 1, 0, 4)
            activate(0, 1)
        if step == 14:
            project(1, 1, 0, 4)
            activate(1, 1)
        if step == 15:
            for slot, place in ((0, mx), (1, partner)):
                t4[place] = tails[mine, slot]
            row_tail()

    def within(j, slot):
        for i in range(TILES):
            rows, width = slice(i * TILE, (i + 1) * TILE), (i + 1) * TILE
            scores = lax.dot_general(
                qkv[2, slot, rows, j * DH:(j + 1) * DH], qkv[j, slot, 0:width, 0:DH],
                (((1,), (1,)), ((), ())), preferred_element_type=jnp.float32,
            )
            t = lax.broadcasted_iota(jnp.int32, (TILE, 1), 0) + (bases[slot] + i * TILE)
            s = lax.broadcasted_iota(jnp.int32, (1, width), 1) + bases[slot]
            keep = (s <= t) & (s >= starts[slot, rows])
            weights = jnp.where(keep, scores, 0.0).astype(jnp.bfloat16)
            mixed[slot, rows, j * DH:(j + 1) * DH] = jnp.dot(
                weights, qkv[j, slot, 0:width, DH:2 * DH], preferred_element_type=jnp.float32
            )

    for d in (0, 1):
        pzc(2, d, 3, d, 1).wait_recv()
    for k in range(4):
        qx_mate(2, k, mate).wait_recv()
        qx_forward(2, k, across).wait_recv()
        for slot in (1, 0):
            project(2, slot, k, k + 1)
        if k == 0:
            relay(0).start()
    row_pair()
    activate(2, 1)
    relay(1).start()
    relay(2).start()
    activate(2, 0)
    for slot in (1, 0):
        within(0, slot)
        within(1, slot)
    relay(1).wait_recv()
    relay(2).wait_recv()
    row_first = start_of(mz * (NX * TOK), ends)
    before = jnp.zeros((DH, DH), jnp.float32)
    for d, at in ((1, 3), (3, 4)):
        row = mz - d
        used = (row >= 0) & ((row + 1) * (NX * TOK) - 1 >= row_first)
        before = before + used.astype(jnp.float32) * rt[at]
    for j in range(NX):
        begin = start_of((mz * NX + j) * TOK, ends)
        state = (begin <= mz * (NX * TOK) - 1).astype(jnp.float32) * before
        for i in range(j):
            used = ((mz * NX + i + 1) * TOK - 1 >= begin).astype(jnp.float32)
            state = state + used * t4[i]
        inc_send[j] = state.astype(jnp.bfloat16)
    for slot in (0, 1):
        inc_copy(slot, False).start()
    for slot, place in ((0, mx), (1, partner)):
        inc[mine, slot] = inc_send[place]
    for slot in (0, 1):
        inc_copy(slot, True).wait_recv()

    def finish_tile(slot, i):
        rows = slice(i * TILE, (i + 1) * TILE)
        carried_on = (starts[slot, rows] <= bases[slot]).astype(jnp.float32)
        squares = jnp.zeros((TILE, DH), jnp.float32)
        for j in (0, 1):
            columns = slice(j * DH, (j + 1) * DH)
            carried = jnp.dot(
                qkv[2, slot, rows, columns], inc[j, slot], preferred_element_type=jnp.float32
            )
            value = mixed[slot, rows, columns] + carried * carried_on
            if slot == 0:
                mixed[slot, rows, columns] = value
            else:
                osend[rows, columns] = value.astype(jnp.bfloat16)
            squares = squares + value * value
        for a in range(TILE // DH):
            flipped = squares[a * DH:(a + 1) * DH, :].T
            row = i * (TILE // DH) + a
            sends[slot, row:row + 1, :] = jnp.sum(flipped, axis=0, keepdims=True)

    for slot in (0, 1):
        sends[slot, TOK // DH:8, :] = jnp.zeros((8 - TOK // DH, DH), jnp.float32)
    for i in range(TILES):
        finish_tile(1, i)
        if i:
            out_copy(i - 1).start()
    for k in range(PEERS):
        square_copy(1, k).start()
    out_copy(TILES - 1).start()
    for i in range(TILES):
        finish_tile(0, i)
    for k in range(1, PEERS):
        square_copy(0, k).start()
    gain = gain_ref[...].astype(jnp.float32)
    is_first = (group == 0).astype(jnp.float32)

    def gain_of(first):
        rows = [gain[j:j + 1] * first + gain[2 + j:3 + j] * (1.0 - first) for j in (0, 1)]
        return jnp.concatenate(rows, axis=1)

    own_gain, other_gain = gain_of(is_first), gain_of(1.0 - is_first)
    own_columns = pl.ds(pl.multiple_of(group * WID, WID), WID)
    other_columns = pl.ds(pl.multiple_of((1 - group) * WID, WID), WID)
    for side in (0, 1):
        for k in range(PEERS):
            if side or k:
                square_copy(side, k).wait_recv()
    total = sends[0]
    for index in range(1, 2 * PEERS):
        total = total + sums[index]
    inverse = lax.rsqrt(total / (PEERS * 4 * DH) + 1e-06)
    scales = [
        jnp.broadcast_to(inverse[a:a + 1, :], (DH, DH)).T for a in range(TOK // DH)
    ]

    def write(columns, source, factor, a):
        rows = slice(a * DH, (a + 1) * DH)
        value = source[rows, :].astype(jnp.float32)
        value = jnp.concatenate(
            [value[:, :DH] * scales[a], value[:, DH:] * scales[a]], axis=1
        )
        out_ref[rows, columns] = (value * factor).astype(jnp.bfloat16)

    for a in range(TOK // DH):
        write(own_columns, mixed.at[0], own_gain, a)
    for i in range(TILES):
        out_copy(i).wait_recv()
        for a in (2 * i, 2 * i + 1):
            write(other_columns, orecv, other_gain, a)

    last = UNITS - 1
    px_mate(last, mx).wait_send()
    px_partner(last, mx).wait_send()
    px_forward(last, partner).wait_send()
    for d in (0, 1):
        for s in range(4):
            qz_mine(last, d, s, 0).wait_send()
            qz_other(last, d, s, 0).wait_send()
            for k in (0, 1):
                if s < 3 or k == d:
                    pzc(last, d, s, k, 0).wait_send()
    for k in range(4):
        qx_mate(last, k, mx).wait_send()
        qx_partner(last, k, mx).wait_send()
        qx_forward(last, k, partner).wait_send()
    for j in range(SUBS):
        tok_x(j).wait_send()
        for d in (0, 1):
            tok_y(j, d, 0, 0).wait_send()
            tok_y(j, d, 1, 0).wait_send()
        for delta in (0, 1, -1, 2):
            tok_core(j, delta, False).wait_send()
    for slot in (0, 1):
        tail_copy(slot, mx).wait_send()
        inc_copy(slot, False).wait_send()
    for s in range(3):
        relay(s).wait_send()
    for i in range(TILES):
        out_copy(i).wait_send()
    for side in (0, 1):
        for k in range(PEERS):
            if side or k:
                square_copy(side, k).wait_send()


def shards(tokens, w_query, w_keyval, doc_lengths, norm_gain):
    w_kv = jnp.transpose(w_keyval, (1, 0, 2))
    w_q = jnp.transpose(w_query, (1, 0, 2))
    vmem = pl.BlockSpec(memory_space=pltpu.VMEM)
    smem = pl.BlockSpec(memory_space=pltpu.SMEM)
    anywhere = pl.BlockSpec(memory_space=pl.ANY)

    def dma(*shape):
        return pltpu.SemaphoreType.DMA((2, *shape))

    def units(*shape):
        return pltpu.SemaphoreType.DMA((1 + UNITS, *shape))

    f32, bf16 = jnp.float32, jnp.bfloat16
    return pl.pallas_call(
        kernel,
        out_shape=jax.ShapeDtypeStruct((TOK, 2 * WID), bf16),
        in_specs=[smem, anywhere, anywhere, anywhere, vmem],
        out_specs=vmem,
        scratch_shapes=[
            pltpu.VMEM((UNITS, NZ, NX, ROWS, WID), bf16),
            pltpu.VMEM((UNITS, NZ, QR, WID), bf16),
            pltpu.VMEM((UNITS, PR, WID), bf16),
            pltpu.VMEM((2, TOK, DM), bf16),
            pltpu.VMEM((2, TOK, WID), f32),
            pltpu.VMEM((UNITS, 2, TOK, WID), bf16),
            pltpu.VMEM((2, TOK, 1), jnp.int32),
            pltpu.VMEM((2, 2, DH, DH), f32),
            pltpu.VMEM((NX, DH, DH), f32),
            pltpu.VMEM((5, DH, DH), f32),
            pltpu.VMEM((NX, DH, DH), bf16),
            pltpu.VMEM((2, 2, DH, DH), bf16),
            pltpu.VMEM((2, TOK, WID), f32),
            pltpu.VMEM((2 * PEERS, 8, DH), f32),
            pltpu.VMEM((2, 8, DH), f32),
            pltpu.VMEM((TOK, WID), bf16),
            pltpu.VMEM((TOK, WID), bf16),
            pltpu.SemaphoreType.DMA((10,)),
            units(), units(), units(),
            units(2, 4), units(2, 4), units(2, 4, 2),
            units(4), units(4), units(4),
            dma(SUBS), dma(SUBS, 2, 2), dma(SUBS, NY),
            dma(2), dma(3), dma(2), dma(2, PEERS), dma(TILES),
        ],
        compiler_params=pltpu.CompilerParams(
            collective_id=0, has_side_effects=True, vmem_limit_bytes=62 << 20
        ),
        name="layer",
    )(doc_lengths, tokens, w_kv, w_q, norm_gain.reshape(4, DH))


def solution(mesh):
    grid = Mesh(mesh.devices.reshape(NZ, NX, NY, NC), ("z", "x", "y", "core"))
    seq, fsdp = ("z", "x"), ("y", "core")
    return jax.shard_map(
        shards,
        mesh=grid,
        in_specs=(P(seq, None), P(seq, fsdp, None), P(seq, fsdp, None), P(), P(fsdp)),
        out_specs=P(seq, fsdp),
        check_vma=False,
    )
```
